128 devices in a mesh: dom: 16 (over z, y), qgrp: 8 (over x, core).
Axes of the slice: x: 4, y: 4, z: 4, core: 2. Of those that a mesh axis runs over, the one named last changes fastest.
Arguments:
- pair_state: bfloat16 [4096, 16384], P('dom', 'qgrp'), may hold values from -6 to 6
- cotangent: bfloat16 [4096, 16384], P('dom', 'qgrp'), may hold values from -6 to 6
- msg_weight: bfloat16 [2, 128, 128], replicated, may hold values from -0.5 to 0.5
- self_weight: bfloat16 [2, 128, 128], replicated, may hold values from -0.5 to 0.5
- pre_bias: float32 [2, 128], replicated, may hold values from -4 to 4
- norm_gain: float32 [2, 128], replicated, may hold values from 0.1 to 1.9
- rel_embed: bfloat16 [2, 822, 128], replicated, may hold values from -2 to 2
- rel_ids: int32 [4096, 8], P('dom'), may hold values from 0 to 821
- neighbours: int32 [4096, 8], P('dom'), may hold values from 0 to 384, as said below
- border: int32 [16, 16], P('dom'), may hold values from 0 to 255, as said below
- send_list: int32 [16, 16, 8], P('dom'), may hold values from 0 to 16, as said below
Outputs:
- final_state: bfloat16 [4096, 16384], P('dom', 'qgrp')
- grad_msg: float32 [2, 128, 128], replicated
- grad_self: float32 [2, 128, 128], replicated
- grad_bias: float32 [2, 128], replicated
- grad_gain: float32 [2, 128], replicated
- grad_rel: float32 [2, 822, 128], replicated
The draws below stay inside these ranges and needn't reach their ends.
Inputs may be any that keep to these rules, and one draw needn't show every extreme that they name: `neighbours`: row v of partition d lists its incoming edges: n below 256 is row n of the same partition; 256 + p * 8 + j, with p not d and j below the count of send_list[p, d], is the j-th row that p sends to d; 384 is an empty slot. Each row has 1 to 8 edges, empty slots last. `border`: the 16 boundary rows of a partition are distinct rows of that partition. send_list[p, d] holds count distinct indices into border[p], then the value 16; count is 0 for d = p, 8 for d = (p + 1) mod 16, and 1 to 8 otherwise.
All inputs are finite; a program needn't handle non-finite values.
Results may differ from the reference program's by a relative error of at most 0.0061.
Values may be sent and summed in bfloat16 or wider, within the bound.
A program may use at most 128 MiB of HBM per device.

```python
import math
import jax
import jax.numpy as jnp
from jax import lax

D = 128
REL = 822
QB = 16
E_DEV = 256
DEG = 8
LAYERS = 2
B = 16
SLOT = 8
NENT = 4096
QUERIES = 128
N_DOM = 16
N_QGRP = 8


def border_pick(subkey):
    first_key, second_key = jax.random.split(subkey)
    inner = jax.random.permutation(first_key, E_DEV - 2)[:B - 2] + 1
    rows = jnp.concatenate([jnp.array([0, E_DEV - 1], jnp.int32), inner.astype(jnp.int32)])
    return jax.random.permutation(second_key, rows)


def slot_pick(subkey):
    first_key, second_key = jax.random.split(subkey)
    inner = jax.random.permutation(first_key, B - 1)[:SLOT - 1] + 1
    picks = jnp.concatenate([jnp.zeros((1,), jnp.int32), inner.astype(jnp.int32)])
    return jax.random.permutation(second_key, picks)


def graph_tables(key):
    folded = jax.random.fold_in(key, 4111)
    streams = jax.random.split(folded, 8)
    border_table = jax.vmap(border_pick)(jax.random.split(streams[0], N_DOM)).astype(jnp.int32)
    parts_range = jnp.arange(N_DOM, dtype=jnp.int32)
    counts = jax.random.randint(streams[1], (N_DOM, N_DOM), 1, SLOT + 1)
    counts = jnp.where((parts_range[:, None] + 1) % N_DOM == parts_range[None, :], SLOT, counts)
    counts = jnp.where(parts_range[:, None] == parts_range[None, :], 0, counts)
    chosen = jax.vmap(slot_pick)(jax.random.split(streams[2], N_DOM * N_DOM))
    chosen = chosen.reshape(N_DOM, N_DOM, SLOT)
    slot_lists = jnp.where(jnp.arange(SLOT)[None, None, :] < counts[:, :, None], chosen, B).astype(jnp.int32)
    shape = (N_DOM, E_DEV, DEG)
    receiver = jnp.broadcast_to(parts_range[:, None, None], shape)
    degrees = jax.random.randint(streams[3], (N_DOM, E_DEV, 1), 1, DEG + 1)
    local_pick = jax.random.randint(streams[4], shape, 0, E_DEV)
    source = (receiver + 1 + jax.random.randint(streams[5], shape, 0, N_DOM - 1)) % N_DOM
    available = counts[source, receiver]
    within = jax.random.randint(streams[6], shape, 0, available)
    remote = E_DEV + source * SLOT + within
    is_remote = jax.random.randint(streams[7], shape, 0, 4) == 0
    entries = jnp.where(is_remote, remote, local_pick)
    entries = jnp.where(jnp.arange(DEG)[None, None, :] < degrees, entries, E_DEV + N_DOM * SLOT)
    return (border_table, slot_lists, entries.reshape(N_DOM * E_DEV, DEG).astype(jnp.int32))


def draw_neighbours(key, part):
    return graph_tables(key)[2]


def draw_border(key, part):
    return graph_tables(key)[0]


def draw_send_list(key, part):
    return graph_tables(key)[1]


def plant(values, stream_key, low, top_value):
    extent = values.shape
    place = [jax.random.randint(jax.random.fold_in(stream_key, axis), (), 0, extent[axis]) for axis in range(len(extent))]
    values = values.at[tuple(place)].set(low)
    longest = extent.index(max(extent))
    place[longest] = (place[longest] + 1) % extent[longest]
    return values.at[tuple(place)].set(top_value)


def level_of(stream_key, shape, cuts, low, top_value):
    gain, own = 1.0, jax.random.fold_in(stream_key, 6)
    for dim, blocks in cuts:
        heights = jnp.exp(jax.random.uniform(jax.random.fold_in(own, dim), (blocks,), jnp.float32, low / len(cuts), top_value / len(cuts)))
        gain = gain * jnp.repeat(heights, shape[dim] // blocks).reshape([-1 if axis == dim else 1 for axis in range(len(shape))])
    return gain


def normal_values(rng, dims, spread, reach, cuts=(), held_as=jnp.bfloat16):
    gain = level_of(rng, dims, cuts, -0.22, 0.18) if cuts else 1.0
    values = jax.random.normal(rng, dims, jnp.float32) * spread * gain
    return jnp.minimum(jnp.maximum(values, -reach), reach).astype(held_as)


def setup_inputs(seed: int = 0) -> dict:
    streams_of = jax.random.split(jax.random.key(seed), 12)
    return {
        "pair_state": normal_values(streams_of[0], (NENT, QUERIES * D), 1.0, 6.0, ((0, 16), (1, 8))),
        "cotangent": normal_values(streams_of[1], (NENT, QUERIES * D), 1.0, 6.0, ((0, 16), (1, 8))),
        "msg_weight": normal_values(streams_of[2], (LAYERS, D, D), D ** -0.5, 0.5),
        "self_weight": normal_values(streams_of[3], (LAYERS, D, D), D ** -0.5, 0.5),
        "pre_bias": normal_values(streams_of[4], (LAYERS, D), 1.0, 4.0, (), jnp.float32),
        "norm_gain": jnp.clip(1.0 + 0.18 * jax.random.normal(streams_of[5], (LAYERS, D), jnp.float32), 0.1, 1.9),
        "rel_embed": normal_values(streams_of[6], (LAYERS, REL, D), 0.35, 2.0),
        "rel_ids": plant(jax.random.randint(streams_of[7], (NENT, DEG), 0, REL), jax.random.fold_in(streams_of[7], 1), 0, REL - 1).astype(jnp.int32),
        "neighbours": draw_neighbours(jax.random.fold_in(streams_of[11], 71), 0),
        "border": draw_border(jax.random.fold_in(streams_of[11], 71), 0),
        "send_list": draw_send_list(jax.random.fold_in(streams_of[11], 71), 0),
    }


def gather_messages(table, index, relation, rel_table):
    entity_rows, degree = index.shape
    features = table.shape[1]
    breadth = rel_table.shape[1]
    heads = features // breadth
    block_rows = math.gcd(entity_rows, 256)
    blocks = entity_rows // block_rows

    def one_block(pieces):
        block_index, block_rel = pieces
        sources = table[block_index].astype(jnp.float32).reshape(block_rows, degree, heads, breadth)
        factors = rel_table[block_rel].astype(jnp.float32)
        summed = jnp.einsum('rkqd,rkd->rqd', sources, factors)
        return summed.reshape(block_rows, features).astype(jnp.bfloat16)
    result = lax.map(one_block, (index.reshape(blocks, block_rows, degree), relation.reshape(blocks, block_rows, degree)))
    return result.reshape(entity_rows, features)

def scatter_messages(table, index, relation, rel_table, upstream, with_rows):
    entity_rows, degree = index.shape
    features = table.shape[1]
    breadth = rel_table.shape[1]
    heads = features // breadth
    block_rows = math.gcd(entity_rows, 256)
    blocks = entity_rows // block_rows

    def one_block(carry, pieces):
        grad_table, grad_rel = carry
        block_index, block_rel, block_up = pieces
        sources = table[block_index].astype(jnp.float32).reshape(block_rows, degree, heads, breadth)
        factors = rel_table[block_rel].astype(jnp.float32)
        upper = block_up.reshape(block_rows, heads, breadth)
        per_edge = jnp.einsum('rkqd,rqd->rkd', sources, upper).reshape(block_rows * degree, breadth)
        grad_rel = grad_rel + jax.ops.segment_sum(per_edge, block_rel.reshape(-1), num_segments=rel_table.shape[0])
        if with_rows:
            contrib = (upper[:, None, :, :] * factors[:, :, None, :]).reshape(block_rows * degree, features)
            grad_table = grad_table.at[block_index.reshape(-1)].add(contrib)
        return ((grad_table, grad_rel), None)
    table_rows = table.shape[0] if with_rows else 1
    start = (jnp.zeros((table_rows, features), jnp.float32), jnp.zeros(rel_table.shape, jnp.float32))
    pieces = (index.reshape(blocks, block_rows, degree), relation.reshape(blocks, block_rows, degree), upstream.reshape(blocks, block_rows, features))
    (grad_table, grad_rel), unused = lax.scan(one_block, start, pieces)
    return (grad_table, grad_rel)

def dense_forward(state, agg_low, w_msg, w_self, bias_row, gain_row):
    entity_rows, features = state.shape
    breadth = w_msg.shape[0]
    flat_state = state.reshape(-1, breadth)
    flat_agg = agg_low.reshape(-1, breadth)
    before = jnp.dot(flat_agg, w_msg, preferred_element_type=jnp.float32) + jnp.dot(flat_state, w_self, preferred_element_type=jnp.float32) + bias_row
    centre = before - lax.optimization_barrier(jnp.mean(before, axis=-1, keepdims=True))
    inverse = lax.rsqrt(lax.optimization_barrier(jnp.mean(centre * centre, axis=-1, keepdims=True)) + 1e-05)
    normed = centre * inverse
    scaled = normed * gain_row
    output = (flat_state.astype(jnp.float32) + scaled * jax.nn.sigmoid(scaled)).astype(jnp.bfloat16)
    return (output.reshape(entity_rows, features), (normed, inverse, scaled))

def dense_backward(upstream, state, agg_low, w_msg, w_self, gain_row, saved, need_state):
    normed, inverse, scaled = saved
    entity_rows, features = state.shape
    breadth = w_msg.shape[0]
    flat_state = state.reshape(-1, breadth)
    flat_agg = agg_low.reshape(-1, breadth)
    flat_up = upstream.reshape(-1, breadth)
    logistic = jax.nn.sigmoid(scaled)
    grad_scaled = flat_up * logistic * (1.0 + scaled * (1.0 - logistic))
    grad_gain = lax.optimization_barrier(jnp.sum(grad_scaled * normed, axis=0))
    grad_normed = grad_scaled * gain_row
    grad_pre = inverse * (grad_normed - lax.optimization_barrier(jnp.mean(grad_normed, axis=-1, keepdims=True)) - normed * lax.optimization_barrier(jnp.mean(grad_normed * normed, axis=-1, keepdims=True)))
    grad_bias = lax.optimization_barrier(jnp.sum(grad_pre, axis=0))
    rounded = grad_pre.astype(jnp.bfloat16)
    contract = (((0,), (0,)), ((), ()))
    grad_msg = lax.dot_general(flat_agg, rounded, contract, preferred_element_type=jnp.float32)
    grad_self = lax.dot_general(flat_state, rounded, contract, preferred_element_type=jnp.float32)
    grad_agg = jnp.dot(rounded, w_msg.T, preferred_element_type=jnp.float32).reshape(entity_rows, features)
    grad_state = None
    if need_state:
        grad_state = upstream + jnp.dot(rounded, w_self.T, preferred_element_type=jnp.float32).reshape(entity_rows, features)
    return (grad_gain, grad_bias, grad_msg, grad_self, grad_agg, grad_state)

def global_index(neighbours, border, send_list):
    total_rows = N_DOM * E_DEV
    owners = (jnp.arange(total_rows, dtype=jnp.int32) // E_DEV)[:, None]
    offset = jnp.clip(neighbours - E_DEV, 0, N_DOM * SLOT - 1)
    source = offset // SLOT
    within = offset % SLOT
    picked = jnp.minimum(send_list[source, owners, within], B - 1)
    remote = source * E_DEV + border[source, picked]
    local_row = owners * E_DEV + neighbours
    inner = jnp.where(neighbours < E_DEV + N_DOM * SLOT, remote, total_rows)
    return jnp.where(neighbours < E_DEV, local_row, inner).astype(jnp.int32)

def reference(pair_state, cotangent, msg_weight, self_weight, pre_bias, norm_gain, rel_embed, rel_ids, neighbours, border, send_list):
    total_rows = N_DOM * E_DEV
    features = QB * D
    index = global_index(neighbours, border, send_list)
    states = pair_state.reshape(total_rows, N_QGRP, features).transpose(1, 0, 2)
    cotans = cotangent.reshape(total_rows, N_QGRP, features).transpose(1, 0, 2)
    zero_row = jnp.zeros((1, features), jnp.bfloat16)

    def per_group(pieces):
        state, cotan = pieces
        table_first = jnp.concatenate([state, zero_row])
        agg_first = gather_messages(table_first, index, rel_ids, rel_embed[0])
        middle, saved_first = dense_forward(state, agg_first, msg_weight[0], self_weight[0], pre_bias[0], norm_gain[0])
        table_second = jnp.concatenate([middle, zero_row])
        agg_second = gather_messages(table_second, index, rel_ids, rel_embed[1])
        final, saved_second = dense_forward(middle, agg_second, msg_weight[1], self_weight[1], pre_bias[1], norm_gain[1])
        upstream = cotan.astype(jnp.float32) / QUERIES
        second = dense_backward(upstream, middle, agg_second, msg_weight[1], self_weight[1], norm_gain[1], saved_second, True)
        grad_table, rel_second = scatter_messages(table_second, index, rel_ids, rel_embed[1], second[4], True)
        grad_middle = second[5] + grad_table[:total_rows]
        first = dense_backward(grad_middle, state, agg_first, msg_weight[0], self_weight[0], norm_gain[0], saved_first, False)
        unused, rel_first = scatter_messages(table_first, index, rel_ids, rel_embed[0], first[4], False)
        return (final, jnp.stack([first[2], second[2]]), jnp.stack([first[3], second[3]]), jnp.stack([first[1], second[1]]), jnp.stack([first[0], second[0]]), jnp.stack([rel_first, rel_second]))
    outputs = lax.map(per_group, (states, cotans))
    final_state = outputs[0].transpose(1, 0, 2).reshape(total_rows, N_QGRP * features)
    return (final_state, lax.optimization_barrier(jnp.sum(outputs[1], axis=0)), lax.optimization_barrier(jnp.sum(outputs[2], axis=0)), lax.optimization_barrier(jnp.sum(outputs[3], axis=0)), lax.optimization_barrier(jnp.sum(outputs[4], axis=0)), lax.optimization_barrier(jnp.sum(outputs[5], axis=0)))
```

```python
import functools

import jax
import jax.numpy as jnp
from jax import lax
from jax.experimental import pallas as pl
from jax.experimental.pallas import tpu as pltpu
from jax.sharding import PartitionSpec as P

MESH = pl.DeviceIdType.MESH
F32 = jnp.float32
BF16 = jnp.bfloat16
WIDE = 256


def dot(a, b):
    return jnp.dot(a, b, preferred_element_type=F32)


def dot_nt(a, b):
    return lax.dot_general(a, b, (((1,), (1,)), ((), ())), preferred_element_type=F32)


def dot_tn(a, b):
    return lax.dot_general(a, b, (((0,), (0,)), ((), ())), preferred_element_type=F32)


def one_hot(ids, shape, axis):
    return jnp.where(lax.broadcasted_iota(jnp.int32, shape, axis) == ids, 1.0, 0.0).astype(BF16)


def split_parts(x):
    high = x.astype(BF16)
    low = (x - high.astype(F32)).astype(BF16)
    return jnp.concatenate([high, low], axis=1)


def fold_rows(x):
    return jnp.sum(x.reshape(x.shape[0] // 8, 8, x.shape[1]), axis=0)


def kernel(
    parts,
    groups,
    chunk,
    h_ref,
    cot_ref,
    wm_ref,
    ws_ref,
    bias_ref,
    gain_ref,
    rel_ref,
    relid_ref,
    nb_ref,
    rows_ref,
    final_ref,
    gm_ref,
    gs_ref,
    gb_ref,
    gg_ref,
    gr_ref,
    table,
    hot,
    hot_t,
    rel_t,
    factors,
    rel_cat,
    w_cat,
    ids,
    pick_t,
    kept0,
    kept1,
    contrib,
    xhat0,
    inv0,
    g1,
    agg,
    dagg,
    per_edge,
    grad_w,
    grad_b,
    grad_g,
    stage,
    back_in,
    ar_stage,
    ar_one,
    ar_two_stage,
    ar_two,
    ar_three_stage,
    ar_three,
    send_sems,
    recv_sems,
    ar_send,
    ar_recv,
    ar_send_q,
    ar_recv_q,
):
    me = lax.axis_index("dom")
    meq = lax.axis_index("qgrp")
    rows, features = h_ref.shape
    degree = nb_ref.shape[1]
    breadth = wm_ref.shape[1]
    rel_count = rel_ref.shape[1]
    half_cols = features // 2
    blocks = half_cols // WIDE
    slots = parts * 8
    edges = rows * degree
    rel_rows = rel_cat.shape[0]
    layers = 2
    queries = groups * (features // breadth)

    zero_land = jnp.zeros((slots, half_cols), BF16)
    for half in range(2):
        for layer in range(layers):
            table[layer, half, rows:, :] = zero_land
        back_in[half] = zero_land

    barrier = pltpu.get_barrier_semaphore()

    @pl.loop(1, parts)
    def _(i):
        pl.semaphore_signal(
            barrier, inc=1, device_id={"dom": lax.rem(me + i, parts)}, device_id_type=MESH
        )

    @pl.loop(1, groups)
    def _(i):
        pl.semaphore_signal(
            barrier, inc=1, device_id={"qgrp": lax.rem(meq + i, groups)}, device_id_type=MESH
        )

    pick_t[...] = one_hot(rows_ref[...], (rows, slots), 0)
    pick = jnp.transpose(
        jnp.where(
            lax.broadcasted_iota(jnp.int32, (rows, slots), 0) == rows_ref[...], 1.0, 0.0
        )
    ).astype(BF16)
    for half in range(2):
        stage[0, half] = dot(pick, h_ref[:, half * half_cols : (half + 1) * half_cols]).astype(BF16)

    pl.semaphore_wait(barrier, parts - 1 + groups - 1)

    def exchange(step, half, i, land):
        peer = lax.rem(me + i, parts)
        return pltpu.make_async_remote_copy(
            src_ref=stage.at[step, half, pl.ds(pl.multiple_of(peer * 8, 8), 8)],
            dst_ref=land(pl.multiple_of(me * 8, 8)),
            send_sem=send_sems.at[step, half, i],
            recv_sem=recv_sems.at[step, half, i],
            device_id={"dom": peer},
            device_id_type=MESH,
        )

    def landing(step, half):
        if step < 2:
            return lambda first: table.at[step, half, pl.ds(rows + first, 8)]
        return lambda first: back_in.at[half, pl.ds(first, 8)]

    def send(step, half):
        @pl.loop(1, parts)
        def _(i):
            exchange(step, half, i, landing(step, half)).start()

    def arrive(step, half):
        @pl.loop(1, parts)
        def _(i):
            exchange(step, half, i, landing(step, half)).wait_recv()

    def sent(step, half):
        @pl.loop(1, parts)
        def _(i):
            exchange(step, half, i, landing(step, half)).wait_send()

    send(0, 0)
    send(0, 1)

    for half in range(2):
        table[0, half, :rows, :] = h_ref[:, half * half_cols : (half + 1) * half_cols]
    ids[...] = jnp.zeros_like(ids)
    ids[:, :degree] = nb_ref[...]
    ids[:, degree : 2 * degree] = relid_ref[...]
    ids_t = jnp.transpose(ids[...])
    rel_cat[rel_rows - 96 :, :] = jnp.zeros((96, 2 * breadth), BF16)
    for layer in range(layers):
        rel_cat[:rel_count, layer * breadth : (layer + 1) * breadth] = rel_ref[layer]
        w_cat[layer, :breadth, :] = wm_ref[layer]
        w_cat[layer, breadth:, :] = ws_ref[layer]
    for k in range(degree):
        span = slice(k * rows, (k + 1) * rows)
        hot[span, :] = one_hot(nb_ref[:, k : k + 1], (rows, rows + slots), 1)
        hot_t[:, span] = one_hot(ids_t[k : k + 1, :], (rows + slots, rows), 0)
        rel_t[:, span] = one_hot(ids_t[degree + k : degree + k + 1, :], (rel_rows, rows), 0)
        factors[span, :] = dot(
            one_hot(relid_ref[:, k : k + 1], (rows, rel_rows), 1), rel_cat[...]
        ).astype(BF16)

    grad_w[...] = jnp.zeros_like(grad_w)
    grad_b[...] = jnp.zeros_like(grad_b)
    grad_g[...] = jnp.zeros_like(grad_g)
    per_edge[...] = jnp.zeros_like(per_edge)
    average = jnp.full((2 * breadth, breadth), 1.0 / breadth, BF16)

    def gather(layer, half, cols, kept, agg_cols):
        src = table[layer, half, :, cols]

        @pl.loop(0, degree)
        def _(k):
            span = pl.ds(pl.multiple_of(k * rows, rows), rows)
            kept[span, agg_cols if kept is kept0 else slice(None)] = dot(hot[span, :], src).astype(BF16)

        step = 32

        @pl.loop(0, rows // step)
        def _(r):
            total = None
            for k in range(degree):
                span = pl.ds(pl.multiple_of(k * rows + r * step, step), step)
                source = kept[span, agg_cols if kept is kept0 else slice(None)].astype(F32)
                factor = factors[span, layer * breadth : (layer + 1) * breadth].astype(F32)
                term = source * jnp.concatenate([factor] * (WIDE // breadth), axis=1)
                total = term if total is None else total + term
            agg[layer, pl.ds(pl.multiple_of(r * step, step), step), agg_cols] = total.astype(BF16)

    def forward(layer, x):
        pre = dot(x, w_cat[layer]) + bias_ref[layer : layer + 1, :]
        centre = pre - dot(split_parts(pre), average)
        var = dot((centre * centre).astype(BF16), average[:breadth])
        inv = lax.rsqrt(var + 1e-5)
        return centre * inv, inv

    def activate(layer, xhat):
        y = xhat * gain_ref[layer : layer + 1, :]
        return y, 0.5 * jnp.tanh(0.5 * y) + 0.5

    def backward(layer, up, x, xhat, inv, y, s):
        dy = up * s * (1.0 + y * (1.0 - s))
        dyx = dy * xhat
        grad_g[layer] += fold_rows(dyx)
        gain = gain_ref[layer : layer + 1, :]
        dx = dy * gain
        dxx = dyx * gain
        dpre = inv * (dx - dot(split_parts(dx), average) - xhat * dot(split_parts(dxx), average))
        grad_b[layer] += fold_rows(dpre)
        rounded = dpre.astype(BF16)
        grad_w[layer] += dot_tn(rounded, x)
        return dot_nt(rounded, w_cat[layer])

    def edge_products(kept, cols, layer):
        @pl.loop(0, degree)
        def _(k):
            span = pl.ds(pl.multiple_of(k * rows, rows), rows)
            source = kept[span, cols].astype(F32)
            product = source * dagg[...]
            total = product[:, :breadth]
            for part in range(1, WIDE // breadth):
                total = total + product[:, part * breadth : (part + 1) * breadth]
            per_edge[layer, span, :] += total

    for half in range(2):
        arrive(0, half)

        @pl.loop(0, blocks)
        def _(c):
            cols = pl.ds(pl.multiple_of(c * WIDE, WIDE), WIDE)
            wide = pl.ds(pl.multiple_of(half * half_cols + c * WIDE, WIDE), WIDE)
            gather(0, half, cols, kept0, wide)
            for part in range(WIDE // breadth):
                at = pl.ds(
                    pl.multiple_of(half * half_cols + c * WIDE + part * breadth, breadth), breadth
                )
                mine = pl.ds(pl.multiple_of(c * WIDE + part * breadth, breadth), breadth)
                state = h_ref[:, at]
                x = jnp.concatenate([agg[0, :, at], state], axis=1)
                xhat, inv = forward(0, x)
                xhat0[:, at] = xhat
                inv0[:, at] = inv
                y, s = activate(0, xhat)
                table[1, half, :rows, mine] = (state.astype(F32) + y * s).astype(BF16)

        stage[1, half] = dot(pick_to_rows(pick_t), table[1, half, :rows, :]).astype(BF16)
        send(1, half)

    for half in range(2):
        arrive(1, half)

        @pl.loop(0, blocks)
        def _(c):
            cols = pl.ds(pl.multiple_of(c * WIDE, WIDE), WIDE)
            wide = pl.ds(pl.multiple_of(half * half_cols + c * WIDE, WIDE), WIDE)
            gather(1, half, cols, kept1, wide)
            for part in range(WIDE // breadth):
                at = pl.ds(
                    pl.multiple_of(half * half_cols + c * WIDE + part * breadth, breadth), breadth
                )
                mine = pl.ds(pl.multiple_of(c * WIDE + part * breadth, breadth), breadth)
                state = table[1, half, :rows, mine]
                x = jnp.concatenate([agg[1, :, at], state], axis=1)
                xhat, inv = forward(1, x)
                y, s = activate(1, xhat)
                final_ref[:, at] = (state.astype(F32) + y * s).astype(BF16)
                up = cot_ref[:, at].astype(F32) * (1.0 / queries)
                both = backward(1, up, x, xhat, inv, y, s)
                dagg[:, part * breadth : (part + 1) * breadth] = both[:, :breadth]
                g1[:, at] = up + both[:, breadth:]
            edge_products(kept1, slice(None), 1)

            @pl.loop(0, degree)
            def _(k):
                span = pl.ds(pl.multiple_of(k * rows, rows), rows)
                factor = factors[span, breadth : 2 * breadth].astype(F32)
                contrib[span, :] = (
                    dagg[...] * jnp.concatenate([factor] * (WIDE // breadth), axis=1)
                ).astype(BF16)

            g1[:, wide] += dot(hot_t[:rows, :], contrib[...])
            stage[2, half, :, cols] = dot(hot_t[rows:, :], contrib[...]).astype(BF16)

        send(2, half)

    def gradients(layer):
        ar_stage[layer, :rel_rows, :] = dot(rel_t[...], per_edge[layer].astype(BF16)).astype(BF16)
        for part in range(2):
            first = rel_rows + part * breadth
            ar_stage[layer, first : first + breadth, :] = jnp.transpose(
                grad_w[layer, :, part * breadth : (part + 1) * breadth]
            ).astype(BF16)
        first = rel_rows + 2 * breadth
        ar_stage[layer, first : first + 16, :] = jnp.concatenate(
            [grad_b[layer], grad_g[layer]], axis=0
        ).astype(BF16)
        ar_stage[layer, first + 16 :, :] = jnp.zeros(
            (parts * chunk - first - 16, breadth), BF16
        )

    def scatter_sum(layer, i):
        peer = lax.rem(me + i, parts)
        return pltpu.make_async_remote_copy(
            src_ref=ar_stage.at[layer, pl.ds(pl.multiple_of(peer * chunk, 16), chunk)],
            dst_ref=ar_one.at[layer, me],
            send_sem=ar_send.at[layer, 0, i],
            recv_sem=ar_recv.at[layer, 0, i],
            device_id={"dom": peer},
            device_id_type=MESH,
        )

    def across(layer, i):
        return pltpu.make_async_remote_copy(
            src_ref=ar_two_stage.at[layer],
            dst_ref=ar_two.at[layer, meq],
            send_sem=ar_send_q.at[layer, i],
            recv_sem=ar_recv_q.at[layer, i],
            device_id={"qgrp": lax.rem(meq + i, groups)},
            device_id_type=MESH,
        )

    def spread(layer, i):
        return pltpu.make_async_remote_copy(
            src_ref=ar_three_stage.at[layer],
            dst_ref=ar_three.at[layer, pl.ds(pl.multiple_of(me * chunk, 16), chunk)],
            send_sem=ar_send.at[layer, 1, i],
            recv_sem=ar_recv.at[layer, 1, i],
            device_id={"dom": lax.rem(me + i, parts)},
            device_id_type=MESH,
        )

    def each(count, make, method):
        @pl.loop(1, count)
        def _(i):
            getattr(make(i), method)()

    def reduce_first(layer):
        ar_one[layer, me] = ar_stage[layer, pl.ds(pl.multiple_of(me * chunk, 16), chunk), :]
        each(parts, functools.partial(scatter_sum, layer), "start")

    def reduce_second(layer):
        each(parts, functools.partial(scatter_sum, layer), "wait_recv")
        total = ar_one[layer, 0].astype(F32)
        for p in range(1, parts):
            total = total + ar_one[layer, p].astype(F32)
        ar_two_stage[layer] = total.astype(BF16)
        ar_two[layer, meq] = total.astype(BF16)
        each(groups, functools.partial(across, layer), "start")

    def reduce_third(layer):
        each(groups, functools.partial(across, layer), "wait_recv")
        total = ar_two[layer, 0].astype(F32)
        for p in range(1, groups):
            total = total + ar_two[layer, p].astype(F32)
        ar_three_stage[layer] = total.astype(BF16)
        ar_three[layer, pl.ds(pl.multiple_of(me * chunk, 16), chunk), :] = total.astype(BF16)
        each(parts, functools.partial(spread, layer), "start")

    def reduce_finish(layer):
        each(parts, functools.partial(spread, layer), "wait_recv")
        gr_ref[layer] = ar_three[layer, :rel_count, :].astype(F32)
        gm_ref[layer] = ar_three[layer, rel_rows : rel_rows + breadth, :].astype(F32)
        gs_ref[layer] = ar_three[layer, rel_rows + breadth : rel_rows + 2 * breadth, :].astype(F32)
        first = rel_rows + 2 * breadth
        small = ar_three[layer, first : first + 16, :].astype(F32)
        gb_ref[layer : layer + 1, :] = jnp.sum(small[:8], axis=0, keepdims=True)
        gg_ref[layer : layer + 1, :] = jnp.sum(small[8:], axis=0, keepdims=True)
        each(parts, functools.partial(scatter_sum, layer), "wait_send")
        each(groups, functools.partial(across, layer), "wait_send")
        each(parts, functools.partial(spread, layer), "wait_send")

    gradients(1)
    reduce_first(1)

    for half in range(2):
        arrive(2, half)

        @pl.loop(0, blocks)
        def _(c):
            cols = pl.ds(pl.multiple_of(c * WIDE, WIDE), WIDE)
            wide = pl.ds(pl.multiple_of(half * half_cols + c * WIDE, WIDE), WIDE)
            g1[:, wide] += dot(pick_t[...], back_in[half, :, cols])
            for part in range(WIDE // breadth):
                at = pl.ds(
                    pl.multiple_of(half * half_cols + c * WIDE + part * breadth, breadth), breadth
                )
                x = jnp.concatenate([agg[0, :, at], h_ref[:, at]], axis=1)
                xhat = xhat0[:, at]
                y, s = activate(0, xhat)
                both = backward(0, g1[:, at], x, xhat, inv0[:, at], y, s)
                dagg[:, part * breadth : (part + 1) * breadth] = both[:, :breadth]
            edge_products(kept0, wide, 0)

        if half == 0:
            reduce_second(1)
        else:
            reduce_third(1)

    gradients(0)
    reduce_first(0)
    reduce_second(0)
    reduce_third(0)
    reduce_finish(1)
    reduce_finish(0)
    for step in range(3):
        for half in range(2):
            sent(step, half)


def pick_to_rows(pick_t):
    return jnp.transpose(pick_t[...].astype(F32)).astype(BF16)


def local(
    parts,
    groups,
    pair_state,
    cotangent,
    msg_weight,
    self_weight,
    pre_bias,
    norm_gain,
    rel_embed,
    rel_ids,
    neighbours,
    border,
    send_list,
):
    rows, features = pair_state.shape
    degree = neighbours.shape[1]
    layers, rel_count, breadth = rel_embed.shape
    slots = parts * 8
    half_cols = features // 2
    edges = rows * degree
    rel_rows = -(-rel_count // 128) * 128
    chunk = -(-(rel_rows + 2 * breadth + 16) // (parts * 16)) * 16
    total = parts * chunk
    kept = border.shape[1]
    match = send_list[0][:, :, None] == jnp.arange(kept, dtype=jnp.int32)
    chosen = jnp.sum(jnp.where(match, border[0] + 1, 0), axis=-1) - 1
    chosen = chosen.reshape(1, slots)
    vmem = pl.BlockSpec(memory_space=pltpu.VMEM)
    out_shape = [
        jax.ShapeDtypeStruct((rows, features), BF16),
        jax.ShapeDtypeStruct((layers, breadth, breadth), F32),
        jax.ShapeDtypeStruct((layers, breadth, breadth), F32),
        jax.ShapeDtypeStruct((layers, breadth), F32),
        jax.ShapeDtypeStruct((layers, breadth), F32),
        jax.ShapeDtypeStruct((layers, rel_count, breadth), F32),
    ]
    scratch = [
        pltpu.VMEM((layers, 2, rows + slots, half_cols), BF16),
        pltpu.VMEM((edges, rows + slots), BF16),
        pltpu.VMEM((rows + slots, edges), BF16),
        pltpu.VMEM((rel_rows, edges), BF16),
        pltpu.VMEM((edges, layers * breadth), BF16),
        pltpu.VMEM((rel_rows, layers * breadth), BF16),
        pltpu.VMEM((layers, 2 * breadth, breadth), BF16),
        pltpu.VMEM((rows, 128), jnp.int32),
        pltpu.VMEM((rows, slots), BF16),
        pltpu.VMEM((edges, features), BF16),
        pltpu.VMEM((edges, WIDE), BF16),
        pltpu.VMEM((edges, WIDE), BF16),
        pltpu.VMEM((rows, features), F32),
        pltpu.VMEM((rows, features), F32),
        pltpu.VMEM((rows, features), F32),
        pltpu.VMEM((layers, rows, features), BF16),
        pltpu.VMEM((rows, WIDE), F32),
        pltpu.VMEM((layers, edges, breadth), F32),
        pltpu.VMEM((layers, breadth, 2 * breadth), F32),
        pltpu.VMEM((layers, 8, breadth), F32),
        pltpu.VMEM((layers, 8, breadth), F32),
        pltpu.VMEM((3, 2, slots, half_cols), BF16),
        pltpu.VMEM((2, slots, half_cols), BF16),
        pltpu.VMEM((layers, total, breadth), BF16),
        pltpu.VMEM((layers, parts, chunk, breadth), BF16),
        pltpu.VMEM((layers, chunk, breadth), BF16),
        pltpu.VMEM((layers, groups, chunk, breadth), BF16),
        pltpu.VMEM((layers, chunk, breadth), BF16),
        pltpu.VMEM((layers, total, breadth), BF16),
        pltpu.SemaphoreType.DMA((3, 2, parts)),
        pltpu.SemaphoreType.DMA((3, 2, parts)),
        pltpu.SemaphoreType.DMA((layers, 2, parts)),
        pltpu.SemaphoreType.DMA((layers, 2, parts)),
        pltpu.SemaphoreType.DMA((layers, groups)),
        pltpu.SemaphoreType.DMA((layers, groups)),
    ]
    return tuple(
        pl.pallas_call(
            functools.partial(kernel, parts, groups, chunk),
            out_shape=out_shape,
            in_specs=[vmem] * 10,
            out_specs=[vmem] * 6,
            scratch_shapes=scratch,
            compiler_params=pltpu.CompilerParams(
                collective_id=0, has_side_effects=True, vmem_limit_bytes=67043328
            ),
            name="bellman_ford",
        )(
            pair_state,
            cotangent,
            msg_weight,
            self_weight,
            pre_bias,
            norm_gain,
            rel_embed,
            rel_ids,
            neighbours,
            chosen,
        )
    )


def solution(mesh):
    in_specs = (
        P("dom", "qgrp"),
        P("dom", "qgrp"),
        P(),
        P(),
        P(),
        P(),
        P(),
        P("dom", None),
        P("dom", None),
        P("dom", None),
        P("dom", None, None),
    )
    out_specs = (P("dom", "qgrp"), P(), P(), P(), P(), P())
    run = functools.partial(local, mesh.shape["dom"], mesh.shape["qgrp"])
    return jax.shard_map(run, mesh=mesh, in_specs=in_specs, out_specs=out_specs, check_vma=False)
```

```python
import functools

import jax
import jax.numpy as jnp
from jax import lax
from jax.experimental import pallas as pl
from jax.experimental.pallas import tpu as pltpu
from jax.sharding import PartitionSpec as P

MESH = pl.DeviceIdType.MESH
F32 = jnp.float32
BF16 = jnp.bfloat16
WIDE = 256
STEP = 32
TOGETHER = 8


def dot(a, b):
    return jnp.dot(a, b, preferred_element_type=F32)


def dot_nt(a, b):
    return lax.dot_general(a, b, (((1,), (1,)), ((), ())), preferred_element_type=F32)


def dot_tn(a, b):
    return lax.dot_general(a, b, (((0,), (0,)), ((), ())), preferred_element_type=F32)


def one_hot(ids, shape, axis):
    return jnp.where(lax.broadcasted_iota(jnp.int32, shape, axis) == ids, 1.0, 0.0).astype(BF16)


def place(ids, shape, axis):
    low = lax.broadcasted_iota(jnp.int32, shape, axis) == (ids & 127)
    return jnp.where(low, ids >> 7, -1).astype(F32).astype(BF16)


def tile_hot(placed, tile):
    return jnp.where(placed == jnp.asarray(tile, BF16), jnp.ones_like(placed), jnp.zeros_like(placed))


def mean_row(x):
    return jnp.mean(x, axis=1, keepdims=True)


def fold_rows(x):
    return jnp.sum(x.reshape(x.shape[0] // 8, 8, x.shape[1]), axis=0)


def kernel(
    parts,
    groups,
    chunk,
    h_ref,
    cot_ref,
    wm_ref,
    ws_ref,
    bias_ref,
    gain_ref,
    rel_ref,
    relid_ref,
    nb_ref,
    rows_ref,
    final_ref,
    gm_ref,
    gs_ref,
    gb_ref,
    gg_ref,
    gr_ref,
    table,
    hot,
    hot_t,
    rel_t,
    factors,
    rel_cat,
    w_cat,
    pick,
    pick_t,
    kept0,
    kept1,
    contrib,
    xhat0,
    inv0,
    g1,
    agg,
    dagg,
    per_edge,
    grad_w,
    grad_b,
    grad_g,
    stage,
    back_in,
    ar_stage,
    ar_one,
    ar_two_stage,
    ar_two,
    ar_three_stage,
    ar_three,
    send_sems,
    recv_sems,
    ar_send,
    ar_recv,
    ar_send_q,
    ar_recv_q,
):
    me = lax.axis_index("dom")
    meq = lax.axis_index("qgrp")
    rows, features = h_ref.shape
    degree = nb_ref.shape[1]
    breadth = wm_ref.shape[1]
    rel_count = rel_ref.shape[1]
    half_cols = features // 2
    blocks = half_cols // WIDE
    slots = parts * 8
    edges = rows * degree
    rel_rows = rel_cat.shape[0]
    layers = 2
    chunks = rows // STEP
    group = degree * STEP
    queries = groups * (features // breadth)

    zero_land = jnp.zeros((slots, half_cols), BF16)
    for half in range(2):
        for layer in range(layers):
            table[layer, half, rows:, :] = zero_land
        back_in[half] = zero_land

    barrier = pltpu.get_barrier_semaphore()

    @pl.loop(1, parts)
    def _(i):
        pl.semaphore_signal(
            barrier, inc=1, device_id={"dom": lax.rem(me + i, parts)}, device_id_type=MESH
        )

    @pl.loop(1, groups)
    def _(i):
        pl.semaphore_signal(
            barrier, inc=1, device_id={"qgrp": lax.rem(meq + i, groups)}, device_id_type=MESH
        )

    pick_t[...] = one_hot(rows_ref[...], (rows, slots), 0)
    pick[...] = jnp.transpose(
        jnp.where(
            lax.broadcasted_iota(jnp.int32, (rows, slots), 0) == rows_ref[...], 1.0, 0.0
        )
    ).astype(BF16)
    for half in range(2):
        stage[0, half] = dot(pick[...], h_ref[:, half * half_cols : (half + 1) * half_cols]).astype(BF16)

    pl.semaphore_wait(barrier, parts - 1 + groups - 1)

    def exchange(step, half, i, land):
        peer = lax.rem(me + i, parts)
        return pltpu.make_async_remote_copy(
            src_ref=stage.at[step, half, pl.ds(pl.multiple_of(peer * 8, 8), 8)],
            dst_ref=land(pl.multiple_of(me * 8, 8)),
            send_sem=send_sems.at[step, half, i],
            recv_sem=recv_sems.at[step, half, i],
            device_id={"dom": peer},
            device_id_type=MESH,
        )

    def landing(step, half):
        if step < 2:
            return lambda first: table.at[step, half, pl.ds(rows + first, 8)]
        return lambda first: back_in.at[half, pl.ds(first, 8)]

    def send(step, half):
        @pl.loop(1, parts)
        def _(i):
            exchange(step, half, i, landing(step, half)).start()

    def arrive(step, half):
        @pl.loop(1, parts)
        def _(i):
            exchange(step, half, i, landing(step, half)).wait_recv()

    def sent(step, half):
        @pl.loop(1, parts)
        def _(i):
            exchange(step, half, i, landing(step, half)).wait_send()

    send(0, 0)
    send(0, 1)

    for half in range(2):
        table[0, half, :rows, :] = h_ref[:, half * half_cols : (half + 1) * half_cols]
    rel_cat[rel_rows - 96 :, :] = jnp.zeros((96, 2 * breadth), BF16)
    for layer in range(layers):
        rel_cat[:rel_count, layer * breadth : (layer + 1) * breadth] = rel_ref[layer]
        w_cat[layer, :breadth, :] = wm_ref[layer]
        w_cat[layer, breadth:, :] = ws_ref[layer]
    across_ids = jnp.zeros((group, 128), jnp.int32)
    lanes = lax.broadcasted_iota(jnp.int32, (group, 128), 1)
    for r in range(chunks):
        span = slice(r * group, (r + 1) * group)
        some = slice(r * STEP, (r + 1) * STEP)
        near = jnp.concatenate(
            [jnp.broadcast_to(nb_ref[some, k : k + 1], (STEP, 128)) for k in range(degree)], axis=0
        )
        kind = jnp.concatenate(
            [jnp.broadcast_to(relid_ref[some, k : k + 1], (STEP, 128)) for k in range(degree)], axis=0
        )
        across_ids = jnp.where(lanes == r, near, across_ids)
        across_ids = jnp.where(lanes == chunks + r, kind, across_ids)
        placed = place(near, (group, 128), 1)
        for tile in range((rows + slots) // 128):
            hot[span, tile * 128 : (tile + 1) * 128] = tile_hot(placed, tile)
        placed = place(kind, (group, 128), 1)
        which = jnp.concatenate([tile_hot(placed, t) for t in range(rel_rows // 128)], axis=1)
        factors[span, :] = dot(which, rel_cat[...]).astype(BF16)
    down_ids = jnp.transpose(across_ids)
    for r in range(chunks):
        span = slice(r * group, (r + 1) * group)
        placed = place(down_ids[r : r + 1, :], (128, group), 0)
        for tile in range((rows + slots) // 128):
            hot_t[tile * 128 : (tile + 1) * 128, span] = tile_hot(placed, tile)
        placed = place(down_ids[chunks + r : chunks + r + 1, :], (128, group), 0)
        for tile in range(rel_rows // 128):
            rel_t[tile * 128 : (tile + 1) * 128, span] = tile_hot(placed, tile)

    grad_w[...] = jnp.zeros_like(grad_w)
    grad_b[...] = jnp.zeros_like(grad_b)
    grad_g[...] = jnp.zeros_like(grad_g)
    per_edge[...] = jnp.zeros_like(per_edge)

    def gather(layer, half, cols, kept, agg_cols):
        src = table[layer, half, :, cols]

        at = agg_cols if kept is kept0 else slice(None)
        for first in range(0, chunks, TOGETHER):
            found = dot(hot[first * group : (first + TOGETHER) * group, :], src)
            for r in range(first, first + TOGETHER):
                mine = found[(r - first) * group : (r - first + 1) * group]
                span = slice(r * group, (r + 1) * group)
                kept[span, at] = mine.astype(BF16)
                total = None
                for k in range(degree):
                    edge = slice(r * group + k * STEP, r * group + (k + 1) * STEP)
                    factor = factors[edge, layer * breadth : (layer + 1) * breadth].astype(F32)
                    term = mine[k * STEP : (k + 1) * STEP] * jnp.concatenate(
                        [factor] * (WIDE // breadth), axis=1
                    )
                    total = term if total is None else total + term
                agg[layer, r * STEP : (r + 1) * STEP, agg_cols] = total.astype(BF16)

    def forward(layer, x):
        pre = dot(x, w_cat[layer]) + bias_ref[layer : layer + 1, :]
        centre = pre - mean_row(pre)
        var = mean_row(centre * centre)
        inv = lax.rsqrt(var + 1e-5)
        return centre * inv, inv

    def activate(layer, xhat):
        y = xhat * gain_ref[layer : layer + 1, :]
        return y, 0.5 * jnp.tanh(0.5 * y) + 0.5

    def backward(layer, up, x, xhat, inv, y, s):
        dy = up * s * (1.0 + y * (1.0 - s))
        dyx = dy * xhat
        grad_g[layer] += fold_rows(dyx)
        gain = gain_ref[layer : layer + 1, :]
        dx = dy * gain
        dxx = dyx * gain
        dpre = inv * (dx - mean_row(dx) - xhat * mean_row(dxx))
        grad_b[layer] += fold_rows(dpre)
        rounded = dpre.astype(BF16)
        grad_w[layer] += dot_tn(rounded, x)
        return dot_nt(rounded, w_cat[layer])

    def edge_products(kept, cols, layer):
        @pl.loop(0, chunks)
        def _(r):
            grad = dagg[pl.ds(pl.multiple_of(r * STEP, STEP), STEP), :]
            for k in range(degree):
                span = pl.ds(pl.multiple_of(r * group + k * STEP, STEP), STEP)
                product = kept[span, cols].astype(F32) * grad
                total = product[:, :breadth]
                for part in range(1, WIDE // breadth):
                    total = total + product[:, part * breadth : (part + 1) * breadth]
                per_edge[layer, span, :] += total
                if layer == 1:
                    factor = factors[span, breadth : 2 * breadth].astype(F32)
                    contrib[span, :] = (
                        grad * jnp.concatenate([factor] * (WIDE // breadth), axis=1)
                    ).astype(BF16)

    for half in range(2):
        arrive(0, half)

        @pl.loop(0, blocks)
        def _(c):
            cols = pl.ds(pl.multiple_of(c * WIDE, WIDE), WIDE)
            wide = pl.ds(pl.multiple_of(half * half_cols + c * WIDE, WIDE), WIDE)
            gather(0, half, cols, kept0, wide)
            for part in range(WIDE // breadth):
                at = pl.ds(
                    pl.multiple_of(half * half_cols + c * WIDE + part * breadth, breadth), breadth
                )
                mine = pl.ds(pl.multiple_of(c * WIDE + part * breadth, breadth), breadth)
                state = h_ref[:, at]
                x = jnp.concatenate([agg[0, :, at], state], axis=1)
                xhat, inv = forward(0, x)
                xhat0[:, at] = xhat
                inv0[:, at] = jnp.broadcast_to(inv, (rows, breadth))
                y, s = activate(0, xhat)
                table[1, half, :rows, mine] = (state.astype(F32) + y * s).astype(BF16)

        stage[1, half] = dot(pick[...], table[1, half, :rows, :]).astype(BF16)
        send(1, half)

    for half in range(2):
        arrive(1, half)

        @pl.loop(0, blocks)
        def _(c):
            cols = pl.ds(pl.multiple_of(c * WIDE, WIDE), WIDE)
            wide = pl.ds(pl.multiple_of(half * half_cols + c * WIDE, WIDE), WIDE)
            gather(1, half, cols, kept1, wide)
            for part in range(WIDE // breadth):
                at = pl.ds(
                    pl.multiple_of(half * half_cols + c * WIDE + part * breadth, breadth), breadth
                )
                mine = pl.ds(pl.multiple_of(c * WIDE + part * breadth, breadth), breadth)
                state = table[1, half, :rows, mine]
                x = jnp.concatenate([agg[1, :, at], state], axis=1)
                xhat, inv = forward(1, x)
                y, s = activate(1, xhat)
                final_ref[:, at] = (state.astype(F32) + y * s).astype(BF16)
                up = cot_ref[:, at].astype(F32) * (1.0 / queries)
                both = backward(1, up, x, xhat, inv, y, s)
                dagg[:, part * breadth : (part + 1) * breadth] = both[:, :breadth]
                g1[:, at] = up + both[:, breadth:]
            edge_products(kept1, slice(None), 1)

            g1[:, wide] += dot(hot_t[:rows, :], contrib[...])
            stage[2, half, :, cols] = dot(hot_t[rows:, :], contrib[...]).astype(BF16)

        send(2, half)

    def gradients(layer):
        ar_stage[layer, :rel_rows, :] = dot(rel_t[...], per_edge[layer].astype(BF16)).astype(BF16)
        for part in range(2):
            first = rel_rows + part * breadth
            ar_stage[layer, first : first + breadth, :] = jnp.transpose(
                grad_w[layer, :, part * breadth : (part + 1) * breadth]
            ).astype(BF16)
        first = rel_rows + 2 * breadth
        ar_stage[layer, first : first + 16, :] = jnp.concatenate(
            [grad_b[layer], grad_g[layer]], axis=0
        ).astype(BF16)
        ar_stage[layer, first + 16 :, :] = jnp.zeros(
            (parts * chunk - first - 16, breadth), BF16
        )

    def scatter_sum(layer, i):
        peer = lax.rem(me + i, parts)
        return pltpu.make_async_remote_copy(
            src_ref=ar_stage.at[layer, pl.ds(pl.multiple_of(peer * chunk, 16), chunk)],
            dst_ref=ar_one.at[layer, me],
            send_sem=ar_send.at[layer, 0, i],
            recv_sem=ar_recv.at[layer, 0, i],
            device_id={"dom": peer},
            device_id_type=MESH,
        )

    def across(layer, i):
        return pltpu.make_async_remote_copy(
            src_ref=ar_two_stage.at[layer],
            dst_ref=ar_two.at[layer, meq],
            send_sem=ar_send_q.at[layer, i],
            recv_sem=ar_recv_q.at[layer, i],
            device_id={"qgrp": lax.rem(meq + i, groups)},
            device_id_type=MESH,
        )

    def spread(layer, i):
        return pltpu.make_async_remote_copy(
            src_ref=ar_three_stage.at[layer],
            dst_ref=ar_three.at[layer, pl.ds(pl.multiple_of(me * chunk, 16), chunk)],
            send_sem=ar_send.at[layer, 1, i],
            recv_sem=ar_recv.at[layer, 1, i],
            device_id={"dom": lax.rem(me + i, parts)},
            device_id_type=MESH,
        )

    def each(count, make, method):
        @pl.loop(1, count)
        def _(i):
            getattr(make(i), method)()

    def reduce_first(layer):
        ar_one[layer, me] = ar_stage[layer, pl.ds(pl.multiple_of(me * chunk, 16), chunk), :]
        each(parts, functools.partial(scatter_sum, layer), "start")

    def reduce_second(layer):
        each(parts, functools.partial(scatter_sum, layer), "wait_recv")
        total = ar_one[layer, 0].astype(F32)
        for p in range(1, parts):
            total = total + ar_one[layer, p].astype(F32)
        ar_two_stage[layer] = total.astype(BF16)
        ar_two[layer, meq] = total.astype(BF16)
        each(groups, functools.partial(across, layer), "start")

    def reduce_third(layer):
        each(groups, functools.partial(across, layer), "wait_recv")
        total = ar_two[layer, 0].astype(F32)
        for p in range(1, groups):
            total = total + ar_two[layer, p].astype(F32)
        ar_three_stage[layer] = total.astype(BF16)
        ar_three[layer, pl.ds(pl.multiple_of(me * chunk, 16), chunk), :] = total.astype(BF16)
        each(parts, functools.partial(spread, layer), "start")

    def reduce_finish(layer):
        each(parts, functools.partial(spread, layer), "wait_recv")
        gr_ref[layer] = ar_three[layer, :rel_count, :].astype(F32)
        gm_ref[layer] = ar_three[layer, rel_rows : rel_rows + breadth, :].astype(F32)
        gs_ref[layer] = ar_three[layer, rel_rows + breadth : rel_rows + 2 * breadth, :].astype(F32)
        first = rel_rows + 2 * breadth
        small = ar_three[layer, first : first + 16, :].astype(F32)
        gb_ref[layer : layer + 1, :] = jnp.sum(small[:8], axis=0, keepdims=True)
        gg_ref[layer : layer + 1, :] = jnp.sum(small[8:], axis=0, keepdims=True)
        each(parts, functools.partial(scatter_sum, layer), "wait_send")
        each(groups, functools.partial(across, layer), "wait_send")
        each(parts, functools.partial(spread, layer), "wait_send")

    gradients(1)
    reduce_first(1)

    for half in range(2):
        arrive(2, half)

        @pl.loop(0, blocks)
        def _(c):
            cols = pl.ds(pl.multiple_of(c * WIDE, WIDE), WIDE)
            wide = pl.ds(pl.multiple_of(half * half_cols + c * WIDE, WIDE), WIDE)
            g1[:, wide] += dot(pick_t[...], back_in[half, :, cols])
            for part in range(WIDE // breadth):
                at = pl.ds(
                    pl.multiple_of(half * half_cols + c * WIDE + part * breadth, breadth), breadth
                )
                x = jnp.concatenate([agg[0, :, at], h_ref[:, at]], axis=1)
                xhat = xhat0[:, at]
                y, s = activate(0, xhat)
                both = backward(0, g1[:, at], x, xhat, inv0[:, at], y, s)
                dagg[:, part * breadth : (part + 1) * breadth] = both[:, :breadth]
            edge_products(kept0, wide, 0)

        if half == 0:
            reduce_second(1)
        else:
            reduce_third(1)

    gradients(0)
    reduce_first(0)
    reduce_second(0)
    reduce_third(0)
    reduce_finish(1)
    reduce_finish(0)
    for step in range(3):
        for half in range(2):
            sent(step, half)


def local(
    parts,
    groups,
    pair_state,
    cotangent,
    msg_weight,
    self_weight,
    pre_bias,
    norm_gain,
    rel_embed,
    rel_ids,
    neighbours,
    border,
    send_list,
):
    rows, features = pair_state.shape
    degree = neighbours.shape[1]
    layers, rel_count, breadth = rel_embed.shape
    slots = parts * 8
    half_cols = features // 2
    edges = rows * degree
    rel_rows = -(-rel_count // 128) * 128
    chunk = -(-(rel_rows + 2 * breadth + 16) // (parts * 16)) * 16
    total = parts * chunk
    kept = border.shape[1]
    match = send_list[0][:, :, None] == jnp.arange(kept, dtype=jnp.int32)
    chosen = jnp.sum(jnp.where(match, border[0] + 1, 0), axis=-1) - 1
    chosen = chosen.reshape(1, slots)
    vmem = pl.BlockSpec(memory_space=pltpu.VMEM)
    out_shape = [
        jax.ShapeDtypeStruct((rows, features), BF16),
        jax.ShapeDtypeStruct((layers, breadth, breadth), F32),
        jax.ShapeDtypeStruct((layers, breadth, breadth), F32),
        jax.ShapeDtypeStruct((layers, breadth), F32),
        jax.ShapeDtypeStruct((layers, breadth), F32),
        jax.ShapeDtypeStruct((layers, rel_count, breadth), F32),
    ]
    scratch = [
        pltpu.VMEM((layers, 2, rows + slots, half_cols), BF16),
        pltpu.VMEM((edges, rows + slots), BF16),
        pltpu.VMEM((rows + slots, edges), BF16),
        pltpu.VMEM((rel_rows, edges), BF16),
        pltpu.VMEM((edges, layers * breadth), BF16),
        pltpu.VMEM((rel_rows, layers * breadth), BF16),
        pltpu.VMEM((layers, 2 * breadth, breadth), BF16),
        pltpu.VMEM((slots, rows), BF16),
        pltpu.VMEM((rows, slots), BF16),
        pltpu.VMEM((edges, features), BF16),
        pltpu.VMEM((edges, WIDE), BF16),
        pltpu.VMEM((edges, WIDE), BF16),
        pltpu.VMEM((rows, features), F32),
        pltpu.VMEM((rows, features), F32),
        pltpu.VMEM((rows, features), F32),
        pltpu.VMEM((layers, rows, features), BF16),
        pltpu.VMEM((rows, WIDE), F32),
        pltpu.VMEM((layers, edges, breadth), F32),
        pltpu.VMEM((layers, breadth, 2 * breadth), F32),
        pltpu.VMEM((layers, 8, breadth), F32),
        pltpu.VMEM((layers, 8, breadth), F32),
        pltpu.VMEM((3, 2, slots, half_cols), BF16),
        pltpu.VMEM((2, slots, half_cols), BF16),
        pltpu.VMEM((layers, total, breadth), BF16),
        pltpu.VMEM((layers, parts, chunk, breadth), BF16),
        pltpu.VMEM((layers, chunk, breadth), BF16),
        pltpu.VMEM((layers, groups, chunk, breadth), BF16),
        pltpu.VMEM((layers, chunk, breadth), BF16),
        pltpu.VMEM((layers, total, breadth), BF16),
        pltpu.SemaphoreType.DMA((3, 2, parts)),
        pltpu.SemaphoreType.DMA((3, 2, parts)),
        pltpu.SemaphoreType.DMA((layers, 2, parts)),
        pltpu.SemaphoreType.DMA((layers, 2, parts)),
        pltpu.SemaphoreType.DMA((layers, groups)),
        pltpu.SemaphoreType.DMA((layers, groups)),
    ]
    return tuple(
        pl.pallas_call(
            functools.partial(kernel, parts, groups, chunk),
            out_shape=out_shape,
            in_specs=[vmem] * 10,
            out_specs=[vmem] * 6,
            scratch_shapes=scratch,
            compiler_params=pltpu.CompilerParams(
                collective_id=0, has_side_effects=True, vmem_limit_bytes=67043328
            ),
            name="bellman_ford",
        )(
            pair_state,
            cotangent,
            msg_weight,
            self_weight,
            pre_bias,
            norm_gain,
            rel_embed,
            rel_ids,
            neighbours,
            chosen,
        )
    )


def solution(mesh):
    in_specs = (
        P("dom", "qgrp"),
        P("dom", "qgrp"),
        P(),
        P(),
        P(),
        P(),
        P(),
        P("dom", None),
        P("dom", None),
        P("dom", None),
        P("dom", None, None),
    )
    out_specs = (P("dom", "qgrp"), P(), P(), P(), P(), P())
    run = functools.partial(local, mesh.shape["dom"], mesh.shape["qgrp"])
    return jax.shard_map(run, mesh=mesh, in_specs=in_specs, out_specs=out_specs, check_vma=False)
```

```python
import functools

import jax
import jax.numpy as jnp
from jax import lax
from jax.experimental import pallas as pl
from jax.experimental.pallas import tpu as pltpu
from jax.sharding import PartitionSpec as P

MESH = pl.DeviceIdType.MESH
F32 = jnp.float32
BF16 = jnp.bfloat16
WIDE = 256
STEP = 32
TOGETHER = 2


def dot(a, b):
    return jnp.dot(a, b, preferred_element_type=F32)


def dot_nt(a, b):
    return lax.dot_general(a, b, (((1,), (1,)), ((), ())), preferred_element_type=F32)


def dot_tn(a, b):
    return lax.dot_general(a, b, (((0,), (0,)), ((), ())), preferred_element_type=F32)


def one_hot(ids, shape, axis):
    return jnp.where(lax.broadcasted_iota(jnp.int32, shape, axis) == ids, 1.0, 0.0).astype(BF16)


def place(ids, shape, axis):
    low = lax.broadcasted_iota(jnp.int32, shape, axis) == (ids & 127)
    return jnp.where(low, ids >> 7, -1).astype(F32).astype(BF16)


def tile_hot(placed, tile):
    return jnp.where(placed == jnp.asarray(tile, BF16), jnp.ones_like(placed), jnp.zeros_like(placed))


def mean_row(x):
    return jnp.mean(x, axis=1, keepdims=True)


def fold_rows(x):
    return jnp.sum(x.reshape(x.shape[0] // 8, 8, x.shape[1]), axis=0)


def kernel(
    parts,
    groups,
    chunk,
    h_ref,
    cot_ref,
    wm_ref,
    ws_ref,
    bias_ref,
    gain_ref,
    rel_ref,
    relid_ref,
    nb_ref,
    border_ref,
    send_ref,
    final_ref,
    grads_ref,
    table,
    hot,
    hot_t,
    rel_t,
    factors,
    rel_cat,
    rel_wide,
    w_cat,
    pick,
    pick_t,
    kept0,
    kept1,
    contrib,
    xhat0,
    inv0,
    g1,
    agg,
    dagg,
    per_edge,
    grad_w,
    grad_b,
    grad_g,
    stage,
    back_in,
    ar_stage,
    ar_one,
    ar_two_stage,
    ar_two,
    ar_three_stage,
    ar_three,
    send_sems,
    recv_sems,
    ar_send,
    ar_recv,
    ar_send_q,
    ar_recv_q,
    cot_buf,
    final_buf,
    local_sems,
):
    me = lax.axis_index("dom")
    meq = lax.axis_index("qgrp")
    rows, features = h_ref.shape
    degree = nb_ref.shape[0]
    breadth = wm_ref.shape[1]
    rel_count = rel_ref.shape[0] // 2
    half_cols = features // 2
    blocks = half_cols // WIDE
    slots = parts * 8
    edges = rows * degree
    rel_rows = rel_cat.shape[0]
    layers = 2
    chunks = rows // STEP
    group = degree * STEP
    queries = groups * (features // breadth)

    fetch = pltpu.make_async_copy(cot_ref, cot_buf, local_sems.at[0])
    fetch.start()

    def write_back(half):
        cols = pl.ds(half * half_cols, half_cols)
        return pltpu.make_async_copy(
            final_buf.at[:, cols], final_ref.at[:, cols], local_sems.at[1 + half]
        )

    zero_land = jnp.zeros((slots, half_cols), BF16)
    for half in range(2):
        for layer in range(layers):
            table[layer, half, rows:, :] = zero_land
        back_in[half] = zero_land

    barrier = pltpu.get_barrier_semaphore()

    @pl.loop(1, parts)
    def _(i):
        pl.semaphore_signal(
            barrier, inc=1, device_id={"dom": lax.rem(me + i, parts)}, device_id_type=MESH
        )

    @pl.loop(1, groups)
    def _(i):
        pl.semaphore_signal(
            barrier, inc=1, device_id={"qgrp": lax.rem(meq + i, groups)}, device_id_type=MESH
        )

    lane = lax.broadcasted_iota(jnp.int32, (8, slots), 1)
    repeat = jnp.where(
        lax.broadcasted_iota(jnp.int32, (8, slots), 0) == (lane & 7), 1.0, 0.0
    ).astype(BF16)
    spread_list = dot_tn(send_ref[0].astype(F32).astype(BF16), repeat)
    own = lax.broadcasted_iota(jnp.int32, (parts, slots), 0) == (
        lax.broadcasted_iota(jnp.int32, (parts, slots), 1) >> 3
    )
    place_in_border = jnp.sum(jnp.where(own, spread_list, 0.0), axis=0, keepdims=True)
    kept_rows = border_ref.shape[1]
    chosen = jnp.where(
        lax.broadcasted_iota(jnp.int32, (kept_rows, slots), 0).astype(F32) == place_in_border,
        1.0,
        0.0,
    ).astype(BF16)
    border_rows = jnp.broadcast_to((border_ref[...] + 1).astype(F32), (8, kept_rows)).astype(BF16)
    sent_rows = dot(border_rows, chosen)[:1] - 1.0
    spot = jnp.where(
        lax.broadcasted_iota(jnp.int32, (rows, slots), 0).astype(F32) == sent_rows, 1.0, 0.0
    )
    pick_t[...] = spot.astype(BF16)
    pick[...] = jnp.transpose(spot).astype(BF16)
    for half in range(2):
        stage[0, half] = dot(pick[...], h_ref[:, half * half_cols : (half + 1) * half_cols]).astype(BF16)

    pl.semaphore_wait(barrier, parts - 1 + groups - 1)

    def exchange(step, half, i, land):
        peer = lax.rem(me + i, parts)
        return pltpu.make_async_remote_copy(
            src_ref=stage.at[step, half, pl.ds(pl.multiple_of(peer * 8, 8), 8)],
            dst_ref=land(pl.multiple_of(me * 8, 8)),
            send_sem=send_sems.at[step, half, i],
            recv_sem=recv_sems.at[step, half, i],
            device_id={"dom": peer},
            device_id_type=MESH,
        )

    def landing(step, half):
        if step < 2:
            return lambda first: table.at[step, half, pl.ds(rows + first, 8)]
        return lambda first: back_in.at[half, pl.ds(first, 8)]

    def send(step, half):
        @pl.loop(1, parts)
        def _(i):
            exchange(step, half, i, landing(step, half)).start()

    def arrive(step, half):
        @pl.loop(1, parts)
        def _(i):
            exchange(step, half, i, landing(step, half)).wait_recv()

    def sent(step, half):
        @pl.loop(1, parts)
        def _(i):
            exchange(step, half, i, landing(step, half)).wait_send()

    send(0, 0)
    send(0, 1)

    for half in range(2):
        table[0, half, :rows, :] = h_ref[:, half * half_cols : (half + 1) * half_cols]
    rel_wide[...] = rel_ref[...].astype(F32)
    rel_cat[rel_rows - 96 :, :] = jnp.zeros((96, 2 * breadth), BF16)
    for layer in range(layers):
        rel_cat[:rel_count, layer * breadth : (layer + 1) * breadth] = rel_wide[
            pl.ds(layer, rel_count, stride=2), :
        ].astype(BF16)
        w_cat[layer, :breadth, :] = wm_ref[layer]
        w_cat[layer, breadth:, :] = ws_ref[layer]
    down = jnp.concatenate(
        [nb_ref[...], relid_ref[...], jnp.zeros((128 - 2 * degree, rows), jnp.int32)], axis=0
    )
    columns = jnp.transpose(down)
    across_ids = jnp.zeros((group, 128), jnp.int32)
    lanes = lax.broadcasted_iota(jnp.int32, (group, 128), 1)
    for r in range(chunks):
        span = slice(r * group, (r + 1) * group)
        some = slice(r * STEP, (r + 1) * STEP)
        near = jnp.concatenate(
            [jnp.broadcast_to(columns[some, k : k + 1], (STEP, 128)) for k in range(degree)], axis=0
        )
        kind = jnp.concatenate(
            [
                jnp.broadcast_to(columns[some, degree + k : degree + k + 1], (STEP, 128))
                for k in range(degree)
            ],
            axis=0,
        )
        across_ids = jnp.where(lanes == r, near, across_ids)
        across_ids = jnp.where(lanes == chunks + r, kind, across_ids)
        placed = place(near, (group, 128), 1)
        for tile in range((rows + slots) // 128):
            hot[span, tile * 128 : (tile + 1) * 128] = tile_hot(placed, tile)
        placed = place(kind, (group, 128), 1)
        which = jnp.concatenate([tile_hot(placed, t) for t in range(rel_rows // 128)], axis=1)
        factors[span, :] = dot(which, rel_cat[...]).astype(BF16)
    down_ids = jnp.transpose(across_ids)
    for r in range(chunks):
        span = slice(r * group, (r + 1) * group)
        placed = place(down_ids[r : r + 1, :], (128, group), 0)
        for tile in range((rows + slots) // 128):
            hot_t[tile * 128 : (tile + 1) * 128, span] = tile_hot(placed, tile)
        placed = place(down_ids[chunks + r : chunks + r + 1, :], (128, group), 0)
        for tile in range(rel_rows // 128):
            rel_t[tile * 128 : (tile + 1) * 128, span] = tile_hot(placed, tile)

    grad_w[...] = jnp.zeros_like(grad_w)
    grad_b[...] = jnp.zeros_like(grad_b)
    grad_g[...] = jnp.zeros_like(grad_g)
    per_edge[...] = jnp.zeros_like(per_edge)

    def gather(layer, half, cols, kept, agg_cols):
        src = table[layer, half, :, cols]

        at = agg_cols if kept is kept0 else slice(None)
        for first in range(0, chunks, TOGETHER):
            found = dot(hot[first * group : (first + TOGETHER) * group, :], src)
            for r in range(first, first + TOGETHER):
                mine = found[(r - first) * group : (r - first + 1) * group]
                span = slice(r * group, (r + 1) * group)
                kept[span, at] = mine.astype(BF16)
                total = None
                for k in range(degree):
                    edge = slice(r * group + k * STEP, r * group + (k + 1) * STEP)
                    factor = factors[edge, layer * breadth : (layer + 1) * breadth].astype(F32)
                    term = mine[k * STEP : (k + 1) * STEP] * jnp.concatenate(
                        [factor] * (WIDE // breadth), axis=1
                    )
                    total = term if total is None else total + term
                agg[layer, r * STEP : (r + 1) * STEP, agg_cols] = total.astype(BF16)

    def forward(layer, x):
        pre = dot(x, w_cat[layer]) + bias_ref[layer : layer + 1, :]
        centre = pre - mean_row(pre)
        var = mean_row(centre * centre)
        inv = lax.rsqrt(var + 1e-5)
        return centre * inv, inv

    def activate(layer, xhat):
        y = xhat * gain_ref[layer : layer + 1, :]
        return y, 0.5 * jnp.tanh(0.5 * y) + 0.5

    def backward(layer, up, x, xhat, inv, y, s):
        dy = up * s * (1.0 + y * (1.0 - s))
        dyx = dy * xhat
        grad_g[layer] += fold_rows(dyx)
        gain = gain_ref[layer : layer + 1, :]
        dx = dy * gain
        dxx = dyx * gain
        dpre = inv * (dx - mean_row(dx) - xhat * mean_row(dxx))
        grad_b[layer] += fold_rows(dpre)
        rounded = dpre.astype(BF16)
        grad_w[layer] += dot_tn(rounded, x)
        return dot_nt(rounded, w_cat[layer])

    def edge_products(kept, cols, layer):
        @pl.loop(0, chunks)
        def _(r):
            grad = dagg[pl.ds(pl.multiple_of(r * STEP, STEP), STEP), :]
            for k in range(degree):
                span = pl.ds(pl.multiple_of(r * group + k * STEP, STEP), STEP)
                product = kept[span, cols].astype(F32) * grad
                total = product[:, :breadth]
                for part in range(1, WIDE // breadth):
                    total = total + product[:, part * breadth : (part + 1) * breadth]
                per_edge[layer, span, :] += total
                if layer == 1:
                    factor = factors[span, breadth : 2 * breadth].astype(F32)
                    contrib[span, :] = (
                        grad * jnp.concatenate([factor] * (WIDE // breadth), axis=1)
                    ).astype(BF16)

    for half in range(2):
        arrive(0, half)

        @pl.loop(0, blocks)
        def _(c):
            cols = pl.ds(pl.multiple_of(c * WIDE, WIDE), WIDE)
            wide = pl.ds(pl.multiple_of(half * half_cols + c * WIDE, WIDE), WIDE)
            gather(0, half, cols, kept0, wide)
            for part in range(WIDE // breadth):
                at = pl.ds(
                    pl.multiple_of(half * half_cols + c * WIDE + part * breadth, breadth), breadth
                )
                mine = pl.ds(pl.multiple_of(c * WIDE + part * breadth, breadth), breadth)
                state = h_ref[:, at]
                x = jnp.concatenate([agg[0, :, at], state], axis=1)
                xhat, inv = forward(0, x)
                xhat0[:, at] = xhat
                inv0[:, at] = jnp.broadcast_to(inv, (rows, breadth))
                y, s = activate(0, xhat)
                table[1, half, :rows, mine] = (state.astype(F32) + y * s).astype(BF16)

        stage[1, half] = dot(pick[...], table[1, half, :rows, :]).astype(BF16)
        send(1, half)

    fetch.wait()
    for half in range(2):
        arrive(1, half)

        @pl.loop(0, blocks)
        def _(c):
            cols = pl.ds(pl.multiple_of(c * WIDE, WIDE), WIDE)
            wide = pl.ds(pl.multiple_of(half * half_cols + c * WIDE, WIDE), WIDE)
            gather(1, half, cols, kept1, wide)
            for part in range(WIDE // breadth):
                at = pl.ds(
                    pl.multiple_of(half * half_cols + c * WIDE + part * breadth, breadth), breadth
                )
                mine = pl.ds(pl.multiple_of(c * WIDE + part * breadth, breadth), breadth)
                state = table[1, half, :rows, mine]
                x = jnp.concatenate([agg[1, :, at], state], axis=1)
                xhat, inv = forward(1, x)
                y, s = activate(1, xhat)
                final_buf[:, at] = (state.astype(F32) + y * s).astype(BF16)
                up = cot_buf[:, at].astype(F32) * (1.0 / queries)
                both = backward(1, up, x, xhat, inv, y, s)
                dagg[:, part * breadth : (part + 1) * breadth] = both[:, :breadth]
                g1[:, at] = up + both[:, breadth:]
            edge_products(kept1, slice(None), 1)

            g1[:, wide] += dot(hot_t[:rows, :], contrib[...])
            stage[2, half, :, cols] = dot(hot_t[rows:, :], contrib[...]).astype(BF16)

        send(2, half)
        write_back(half).start()

    def gradients(layer):
        ar_stage[layer, :rel_rows, :] = dot(rel_t[...], per_edge[layer].astype(BF16)).astype(BF16)
        for part in range(2):
            first = rel_rows + part * breadth
            ar_stage[layer, first : first + breadth, :] = jnp.transpose(
                grad_w[layer, :, part * breadth : (part + 1) * breadth]
            ).astype(BF16)
        first = rel_rows + 2 * breadth
        ar_stage[layer, first : first + 16, :] = jnp.concatenate(
            [grad_b[layer], grad_g[layer]], axis=0
        ).astype(BF16)
        ar_stage[layer, first + 16 :, :] = jnp.zeros(
            (parts * chunk - first - 16, breadth), BF16
        )

    def scatter_sum(layer, i):
        peer = lax.rem(me + i, parts)
        return pltpu.make_async_remote_copy(
            src_ref=ar_stage.at[layer, pl.ds(pl.multiple_of(peer * chunk, 16), chunk)],
            dst_ref=ar_one.at[layer, me],
            send_sem=ar_send.at[layer, 0, i],
            recv_sem=ar_recv.at[layer, 0, i],
            device_id={"dom": peer},
            device_id_type=MESH,
        )

    def across(layer, i):
        return pltpu.make_async_remote_copy(
            src_ref=ar_two_stage.at[layer],
            dst_ref=ar_two.at[layer, meq],
            send_sem=ar_send_q.at[layer, i],
            recv_sem=ar_recv_q.at[layer, i],
            device_id={"qgrp": lax.rem(meq + i, groups)},
            device_id_type=MESH,
        )

    def spread(layer, i):
        return pltpu.make_async_remote_copy(
            src_ref=ar_three_stage.at[layer],
            dst_ref=ar_three.at[layer, pl.ds(pl.multiple_of(me * chunk, 16), chunk)],
            send_sem=ar_send.at[layer, 1, i],
            recv_sem=ar_recv.at[layer, 1, i],
            device_id={"dom": lax.rem(me + i, parts)},
            device_id_type=MESH,
        )

    def each(count, make, method):
        @pl.loop(1, count)
        def _(i):
            getattr(make(i), method)()

    def reduce_first(layer):
        ar_one[layer, me] = ar_stage[layer, pl.ds(pl.multiple_of(me * chunk, 16), chunk), :]
        each(parts, functools.partial(scatter_sum, layer), "start")

    def reduce_second(layer):
        each(parts, functools.partial(scatter_sum, layer), "wait_recv")
        total = ar_one[layer, 0].astype(F32)
        for p in range(1, parts):
            total = total + ar_one[layer, p].astype(F32)
        ar_two_stage[layer] = total.astype(BF16)
        ar_two[layer, meq] = total.astype(BF16)
        each(groups, functools.partial(across, layer), "start")

    def reduce_third(layer):
        each(groups, functools.partial(across, layer), "wait_recv")
        total = ar_two[layer, 0].astype(F32)
        for p in range(1, groups):
            total = total + ar_two[layer, p].astype(F32)
        ar_three_stage[layer] = total.astype(BF16)
        ar_three[layer, pl.ds(pl.multiple_of(me * chunk, 16), chunk), :] = total.astype(BF16)
        each(parts, functools.partial(spread, layer), "start")

    def reduce_finish(layer):
        each(parts, functools.partial(spread, layer), "wait_recv")
        grads_ref[layer] = ar_three[layer]
        each(parts, functools.partial(scatter_sum, layer), "wait_send")
        each(groups, functools.partial(across, layer), "wait_send")
        each(parts, functools.partial(spread, layer), "wait_send")

    gradients(1)
    reduce_first(1)

    for half in range(2):
        arrive(2, half)

        @pl.loop(0, blocks)
        def _(c):
            cols = pl.ds(pl.multiple_of(c * WIDE, WIDE), WIDE)
            wide = pl.ds(pl.multiple_of(half * half_cols + c * WIDE, WIDE), WIDE)
            g1[:, wide] += dot(pick_t[...], back_in[half, :, cols])
            for part in range(WIDE // breadth):
                at = pl.ds(
                    pl.multiple_of(half * half_cols + c * WIDE + part * breadth, breadth), breadth
                )
                x = jnp.concatenate([agg[0, :, at], h_ref[:, at]], axis=1)
                xhat = xhat0[:, at]
                y, s = activate(0, xhat)
                both = backward(0, g1[:, at], x, xhat, inv0[:, at], y, s)
                dagg[:, part * breadth : (part + 1) * breadth] = both[:, :breadth]
            edge_products(kept0, wide, 0)

        if half == 0:
            reduce_second(1)
        else:
            reduce_third(1)

    gradients(0)
    reduce_first(0)
    reduce_second(0)
    reduce_third(0)
    reduce_finish(1)
    reduce_finish(0)
    for step in range(3):
        for half in range(2):
            sent(step, half)
    for half in range(2):
        write_back(half).wait()


def unpack(
    final_in,
    grads_in,
    final_out,
    gm_ref,
    gs_ref,
    gb_ref,
    gg_ref,
    gr_ref,
    copy_sem,
):
    whole = pltpu.make_async_copy(final_in, final_out, copy_sem)
    whole.start()
    breadth = gm_ref.shape[1]
    rel_count = gr_ref.shape[0] // 2
    rel_rows = -(-rel_count // 128) * 128
    for layer in range(2):
        gr_ref[pl.ds(layer, rel_count, stride=2), :] = grads_in[layer, :rel_count, :].astype(F32)
        gm_ref[layer] = grads_in[layer, rel_rows : rel_rows + breadth, :].astype(F32)
        gs_ref[layer] = grads_in[layer, rel_rows + breadth : rel_rows + 2 * breadth, :].astype(F32)
        first = rel_rows + 2 * breadth
        small = grads_in[layer, first : first + 16, :].astype(F32)
        gb_ref[layer : layer + 1, :] = jnp.sum(small[:8], axis=0, keepdims=True)
        gg_ref[layer : layer + 1, :] = jnp.sum(small[8:], axis=0, keepdims=True)
    whole.wait()


def local(
    parts,
    groups,
    pair_state,
    cotangent,
    msg_weight,
    self_weight,
    pre_bias,
    norm_gain,
    rel_embed,
    rel_ids,
    neighbours,
    border,
    send_list,
):
    rows, features = pair_state.shape
    degree = neighbours.shape[1]
    layers, rel_count, breadth = rel_embed.shape
    slots = parts * 8
    half_cols = features // 2
    edges = rows * degree
    rel_rows = -(-rel_count // 128) * 128
    chunk = -(-(rel_rows + 2 * breadth + 16) // (parts * 16)) * 16
    total = parts * chunk
    vmem = pl.BlockSpec(memory_space=pltpu.VMEM)
    anywhere = pl.BlockSpec(memory_space=pl.ANY)
    grads_shape = jax.ShapeDtypeStruct((layers, total, breadth), BF16)
    out_shape = [
        jax.ShapeDtypeStruct((rows, features), BF16),
        jax.ShapeDtypeStruct((layers, breadth, breadth), F32),
        jax.ShapeDtypeStruct((layers, breadth, breadth), F32),
        jax.ShapeDtypeStruct((layers, breadth), F32),
        jax.ShapeDtypeStruct((layers, breadth), F32),
        jax.ShapeDtypeStruct((layers * rel_count, breadth), F32),
    ]
    scratch = [
        pltpu.VMEM((layers, 2, rows + slots, half_cols), BF16),
        pltpu.VMEM((edges, rows + slots), BF16),
        pltpu.VMEM((rows + slots, edges), BF16),
        pltpu.VMEM((rel_rows, edges), BF16),
        pltpu.VMEM((edges, layers * breadth), BF16),
        pltpu.VMEM((rel_rows, layers * breadth), BF16),
        pltpu.VMEM((layers * rel_count, breadth), F32),
        pltpu.VMEM((layers, 2 * breadth, breadth), BF16),
        pltpu.VMEM((slots, rows), BF16),
        pltpu.VMEM((rows, slots), BF16),
        pltpu.VMEM((edges, features), BF16),
        pltpu.VMEM((edges, WIDE), BF16),
        pltpu.VMEM((edges, WIDE), BF16),
        pltpu.VMEM((rows, features), F32),
        pltpu.VMEM((rows, features), F32),
        pltpu.VMEM((rows, features), F32),
        pltpu.VMEM((layers, rows, features), BF16),
        pltpu.VMEM((rows, WIDE), F32),
        pltpu.VMEM((layers, edges, breadth), F32),
        pltpu.VMEM((layers, breadth, 2 * breadth), F32),
        pltpu.VMEM((layers, 8, breadth), F32),
        pltpu.VMEM((layers, 8, breadth), F32),
        pltpu.VMEM((3, 2, slots, half_cols), BF16),
        pltpu.VMEM((2, slots, half_cols), BF16),
        pltpu.VMEM((layers, total, breadth), BF16),
        pltpu.VMEM((layers, parts, chunk, breadth), BF16),
        pltpu.VMEM((layers, chunk, breadth), BF16),
        pltpu.VMEM((layers, groups, chunk, breadth), BF16),
        pltpu.VMEM((layers, chunk, breadth), BF16),
        pltpu.VMEM((layers, total, breadth), BF16),
        pltpu.SemaphoreType.DMA((3, 2, parts)),
        pltpu.SemaphoreType.DMA((3, 2, parts)),
        pltpu.SemaphoreType.DMA((layers, 2, parts)),
        pltpu.SemaphoreType.DMA((layers, 2, parts)),
        pltpu.SemaphoreType.DMA((layers, groups)),
        pltpu.SemaphoreType.DMA((layers, groups)),
        pltpu.VMEM((rows, features), BF16),
        pltpu.VMEM((rows, features), BF16),
        pltpu.SemaphoreType.DMA((3,)),
    ]
    final, grads = pl.pallas_call(
        functools.partial(kernel, parts, groups, chunk),
        out_shape=[out_shape[0], grads_shape],
        in_specs=[vmem, anywhere] + [vmem] * 9,
        out_specs=[anywhere, vmem],
        scratch_shapes=scratch,
        compiler_params=pltpu.CompilerParams(
            collective_id=0, has_side_effects=True, vmem_limit_bytes=67043328
        ),
        name="bellman_ford",
    )(
        pair_state,
        cotangent,
        msg_weight,
        self_weight,
        pre_bias,
        norm_gain,
        jnp.transpose(rel_embed, (1, 0, 2)).reshape(layers * rel_count, breadth),
        rel_ids.T,
        neighbours.T,
        border,
        jnp.transpose(send_list, (0, 2, 1)),
    )
    final, gm, gs, gb, gg, gr = pl.pallas_call(
        unpack,
        out_shape=out_shape,
        in_specs=[vmem] * 2,
        out_specs=[anywhere] + [vmem] * 5,
        scratch_shapes=[pltpu.SemaphoreType.DMA],
        compiler_params=pltpu.CompilerParams(vmem_limit_bytes=16 * 1024 * 1024),
        name="unpack",
    )(final, grads)
    return final, gm, gs, gb, gg, jnp.transpose(gr.reshape(rel_count, layers, breadth), (1, 0, 2))


def solution(mesh):
    in_specs = (
        P("dom", "qgrp"),
        P("dom", "qgrp"),
        P(),
        P(),
        P(),
        P(),
        P(),
        P("dom", None),
        P("dom", None),
        P("dom", None),
        P("dom", None, None),
    )
    out_specs = (P("dom", "qgrp"), P(), P(), P(), P(), P())
    run = functools.partial(local, mesh.shape["dom"], mesh.shape["qgrp"])
    return jax.shard_map(run, mesh=mesh, in_specs=in_specs, out_specs=out_specs, check_vma=False)
```

```python
import functools

import jax
import jax.numpy as jnp
from jax import lax
from jax.experimental import pallas as pl
from jax.experimental.pallas import tpu as pltpu
from jax.sharding import PartitionSpec as P

MESH = pl.DeviceIdType.MESH
F32 = jnp.float32
BF16 = jnp.bfloat16
WIDE = 256
STEP = 32
TOGETHER = 4


def dot(a, b):
    return jnp.dot(a, b, preferred_element_type=F32)


def dot_nt(a, b):
    return lax.dot_general(a, b, (((1,), (1,)), ((), ())), preferred_element_type=F32)


def dot_tn(a, b):
    return lax.dot_general(a, b, (((0,), (0,)), ((), ())), preferred_element_type=F32)


def one_hot(ids, shape, axis):
    return jnp.where(lax.broadcasted_iota(jnp.int32, shape, axis) == ids, 1.0, 0.0).astype(BF16)


def place(ids, shape, axis):
    low = lax.broadcasted_iota(jnp.int32, shape, axis) == (ids & 127)
    return jnp.where(low, ids >> 7, -1).astype(F32).astype(BF16)


def tile_hot(placed, tile):
    return jnp.where(placed == jnp.asarray(tile, BF16), jnp.ones_like(placed), jnp.zeros_like(placed))


def mean_row(x):
    return jnp.mean(x, axis=1, keepdims=True)


def fold_rows(x):
    return jnp.sum(x.reshape(x.shape[0] // 8, 8, x.shape[1]), axis=0)


def kernel(
    parts,
    groups,
    chunk,
    h_ref,
    cot_ref,
    wm_ref,
    ws_ref,
    bias_ref,
    gain_ref,
    rel_ref,
    relid_ref,
    nb_ref,
    border_ref,
    send_ref,
    final_ref,
    grads_ref,
    table,
    hot,
    hot_t,
    rel_t,
    factors,
    rel_cat,
    w_cat,
    pick,
    pick_t,
    kept0,
    kept1,
    contrib,
    xhat0,
    inv0,
    g1,
    agg,
    dagg,
    per_edge,
    grad_w,
    grad_b,
    grad_g,
    stage,
    back_in,
    ar_stage,
    ar_one,
    ar_two_stage,
    ar_two,
    ar_three_stage,
    ar_three,
    send_sems,
    recv_sems,
    ar_send,
    ar_recv,
    ar_send_q,
    ar_recv_q,
    cot_buf,
    final_buf,
    local_sems,
):
    me = lax.axis_index("dom")
    meq = lax.axis_index("qgrp")
    rows, features = h_ref.shape
    degree = nb_ref.shape[0]
    breadth = wm_ref.shape[1]
    rel_count = rel_ref.shape[0]
    half_cols = features // 2
    blocks = half_cols // WIDE
    slots = parts * 8
    edges = rows * degree
    rel_rows = rel_cat.shape[0]
    layers = 2
    chunks = rows // STEP
    group = degree * STEP
    queries = groups * (features // breadth)

    fetch = pltpu.make_async_copy(cot_ref, cot_buf, local_sems.at[0])
    fetch.start()

    def write_back(half):
        cols = pl.ds(half * half_cols, half_cols)
        return pltpu.make_async_copy(
            final_buf.at[:, cols], final_ref.at[:, cols], local_sems.at[1 + half]
        )

    zero_land = jnp.zeros((slots, half_cols), BF16)
    for half in range(2):
        for layer in range(layers):
            table[layer, half, rows:, :] = zero_land
        back_in[half] = zero_land

    barrier = pltpu.get_barrier_semaphore()

    @pl.loop(1, parts)
    def _(i):
        pl.semaphore_signal(
            barrier, inc=1, device_id={"dom": lax.rem(me + i, parts)}, device_id_type=MESH
        )

    @pl.loop(1, groups)
    def _(i):
        pl.semaphore_signal(
            barrier, inc=1, device_id={"qgrp": lax.rem(meq + i, groups)}, device_id_type=MESH
        )

    lane = lax.broadcasted_iota(jnp.int32, (8, slots), 1)
    repeat = jnp.where(
        lax.broadcasted_iota(jnp.int32, (8, slots), 0) == (lane & 7), 1.0, 0.0
    ).astype(BF16)
    spread_list = dot_tn(send_ref[0].astype(F32).astype(BF16), repeat)
    own = lax.broadcasted_iota(jnp.int32, (parts, slots), 0) == (
        lax.broadcasted_iota(jnp.int32, (parts, slots), 1) >> 3
    )
    place_in_border = jnp.sum(jnp.where(own, spread_list, 0.0), axis=0, keepdims=True)
    kept_rows = border_ref.shape[1]
    chosen = jnp.where(
        lax.broadcasted_iota(jnp.int32, (kept_rows, slots), 0).astype(F32) == place_in_border,
        1.0,
        0.0,
    ).astype(BF16)
    border_rows = jnp.broadcast_to((border_ref[...] + 1).astype(F32), (8, kept_rows)).astype(BF16)
    sent_rows = dot(border_rows, chosen)[:1] - 1.0
    spot = jnp.where(
        lax.broadcasted_iota(jnp.int32, (rows, slots), 0).astype(F32) == sent_rows, 1.0, 0.0
    )
    pick_t[...] = spot.astype(BF16)
    pick[...] = jnp.transpose(spot).astype(BF16)
    for half in range(2):
        stage[0, half] = dot(pick[...], h_ref[:, half * half_cols : (half + 1) * half_cols]).astype(BF16)

    pl.semaphore_wait(barrier, parts - 1 + groups - 1)

    def exchange(step, half, i, land):
        peer = lax.rem(me + i, parts)
        return pltpu.make_async_remote_copy(
            src_ref=stage.at[step, half, pl.ds(pl.multiple_of(peer * 8, 8), 8)],
            dst_ref=land(pl.multiple_of(me * 8, 8)),
            send_sem=send_sems.at[step, half, i],
            recv_sem=recv_sems.at[step, half, i],
            device_id={"dom": peer},
            device_id_type=MESH,
        )

    def landing(step, half):
        if step < 2:
            return lambda first: table.at[step, half, pl.ds(rows + first, 8)]
        return lambda first: back_in.at[half, pl.ds(first, 8)]

    def send(step, half):
        @pl.loop(1, parts)
        def _(i):
            exchange(step, half, i, landing(step, half)).start()

    def arrive(step, half):
        @pl.loop(1, parts)
        def _(i):
            exchange(step, half, i, landing(step, half)).wait_recv()

    def sent(step, half):
        @pl.loop(1, parts)
        def _(i):
            exchange(step, half, i, landing(step, half)).wait_send()

    send(0, 0)
    send(0, 1)

    for half in range(2):
        table[0, half, :rows, :] = h_ref[:, half * half_cols : (half + 1) * half_cols]
    rel_cat[rel_rows - 96 :, :] = jnp.zeros((96, 2 * breadth), BF16)
    for layer in range(layers):
        rel_cat[:rel_count, layer * breadth : (layer + 1) * breadth] = rel_ref[:, layer, :]
        w_cat[layer, :breadth, :] = wm_ref[layer]
        w_cat[layer, breadth:, :] = ws_ref[layer]
    down = jnp.concatenate(
        [nb_ref[...], relid_ref[...], jnp.zeros((128 - 2 * degree, rows), jnp.int32)], axis=0
    )
    columns = jnp.transpose(down)
    across_ids = jnp.zeros((group, 128), jnp.int32)
    lanes = lax.broadcasted_iota(jnp.int32, (group, 128), 1)
    for r in range(chunks):
        span = slice(r * group, (r + 1) * group)
        some = slice(r * STEP, (r + 1) * STEP)
        near = jnp.concatenate(
            [jnp.broadcast_to(columns[some, k : k + 1], (STEP, 128)) for k in range(degree)], axis=0
        )
        kind = jnp.concatenate(
            [
                jnp.broadcast_to(columns[some, degree + k : degree + k + 1], (STEP, 128))
                for k in range(degree)
            ],
            axis=0,
        )
        across_ids = jnp.where(lanes == r, near, across_ids)
        across_ids = jnp.where(lanes == chunks + r, kind, across_ids)
        placed = place(near, (group, 128), 1)
        for tile in range((rows + slots) // 128):
            hot[span, tile * 128 : (tile + 1) * 128] = tile_hot(placed, tile)
        placed = place(kind, (group, 128), 1)
        which = jnp.concatenate([tile_hot(placed, t) for t in range(rel_rows // 128)], axis=1)
        factors[span, :] = dot(which, rel_cat[...]).astype(BF16)
    down_ids = jnp.transpose(across_ids)
    for r in range(chunks):
        span = slice(r * group, (r + 1) * group)
        placed = place(down_ids[r : r + 1, :], (128, group), 0)
        for tile in range((rows + slots) // 128):
            hot_t[tile * 128 : (tile + 1) * 128, span] = tile_hot(placed, tile)
        placed = place(down_ids[chunks + r : chunks + r + 1, :], (128, group), 0)
        for tile in range(rel_rows // 128):
            rel_t[tile * 128 : (tile + 1) * 128, span] = tile_hot(placed, tile)

    grad_w[...] = jnp.zeros_like(grad_w)
    grad_b[...] = jnp.zeros_like(grad_b)
    grad_g[...] = jnp.zeros_like(grad_g)
    per_edge[...] = jnp.zeros_like(per_edge)

    def gather(layer, half, cols, kept, agg_cols):
        src = table[layer, half, :, cols]

        at = agg_cols if kept is kept0 else slice(None)
        for first in range(0, chunks, TOGETHER):
            found = dot(hot[first * group : (first + TOGETHER) * group, :], src)
            for r in range(first, first + TOGETHER):
                mine = found[(r - first) * group : (r - first + 1) * group]
                span = slice(r * group, (r + 1) * group)
                kept[span, at] = mine.astype(BF16)
                total = None
                for k in range(degree):
                    edge = slice(r * group + k * STEP, r * group + (k + 1) * STEP)
                    factor = factors[edge, layer * breadth : (layer + 1) * breadth].astype(F32)
                    term = mine[k * STEP : (k + 1) * STEP] * jnp.concatenate(
                        [factor] * (WIDE // breadth), axis=1
                    )
                    total = term if total is None else total + term
                agg[layer, r * STEP : (r + 1) * STEP, agg_cols] = total.astype(BF16)

    def forward(layer, x):
        pre = dot(x, w_cat[layer]) + bias_ref[layer : layer + 1, :]
        centre = pre - mean_row(pre)
        var = mean_row(centre * centre)
        inv = lax.rsqrt(var + 1e-5)
        return centre * inv, inv

    def activate(layer, xhat):
        y = xhat * gain_ref[layer : layer + 1, :]
        return y, 0.5 * jnp.tanh(0.5 * y) + 0.5

    def backward(layer, up, x, xhat, inv, y, s):
        dy = up * s * (1.0 + y * (1.0 - s))
        dyx = dy * xhat
        grad_g[layer] += fold_rows(dyx)
        gain = gain_ref[layer : layer + 1, :]
        dx = dy * gain
        dxx = dyx * gain
        dpre = inv * (dx - mean_row(dx) - xhat * mean_row(dxx))
        grad_b[layer] += fold_rows(dpre)
        rounded = dpre.astype(BF16)
        grad_w[layer] += dot_tn(rounded, x)
        return dot_nt(rounded, w_cat[layer])

    def edge_products(kept, cols, layer):
        def piece(r, first):
            grad = dagg[pl.ds(first(r * STEP), STEP), :]
            for k in range(degree):
                span = pl.ds(first(r * group + k * STEP), STEP)
                product = kept[span, cols].astype(F32) * grad
                total = product[:, :breadth]
                for part in range(1, WIDE // breadth):
                    total = total + product[:, part * breadth : (part + 1) * breadth]
                per_edge[layer, span, :] += total
                if layer == 1:
                    factor = factors[span, breadth : 2 * breadth].astype(F32)
                    contrib[span, :] = (
                        grad * jnp.concatenate([factor] * (WIDE // breadth), axis=1)
                    ).astype(BF16)

        if layer == 1:
            for r in range(chunks):
                piece(r, lambda row: row)
        else:

            @pl.loop(0, chunks)
            def _(r):
                piece(r, lambda row: pl.multiple_of(row, STEP))

    for half in range(2):
        arrive(0, half)

        @pl.loop(0, blocks)
        def _(c):
            cols = pl.ds(pl.multiple_of(c * WIDE, WIDE), WIDE)
            wide = pl.ds(pl.multiple_of(half * half_cols + c * WIDE, WIDE), WIDE)
            gather(0, half, cols, kept0, wide)
            for part in range(WIDE // breadth):
                at = pl.ds(
                    pl.multiple_of(half * half_cols + c * WIDE + part * breadth, breadth), breadth
                )
                mine = pl.ds(pl.multiple_of(c * WIDE + part * breadth, breadth), breadth)
                state = h_ref[:, at]
                x = jnp.concatenate([agg[0, :, at], state], axis=1)
                xhat, inv = forward(0, x)
                xhat0[:, at] = xhat
                inv0[:, at] = jnp.broadcast_to(inv, (rows, breadth))
                y, s = activate(0, xhat)
                table[1, half, :rows, mine] = (state.astype(F32) + y * s).astype(BF16)

        stage[1, half] = dot(pick[...], table[1, half, :rows, :]).astype(BF16)
        send(1, half)

    fetch.wait()
    for half in range(2):
        arrive(1, half)

        @pl.loop(0, blocks)
        def _(c):
            cols = pl.ds(pl.multiple_of(c * WIDE, WIDE), WIDE)
            wide = pl.ds(pl.multiple_of(half * half_cols + c * WIDE, WIDE), WIDE)
            gather(1, half, cols, kept1, wide)
            for part in range(WIDE // breadth):
                at = pl.ds(
                    pl.multiple_of(half * half_cols + c * WIDE + part * breadth, breadth), breadth
                )
                mine = pl.ds(pl.multiple_of(c * WIDE + part * breadth, breadth), breadth)
                state = table[1, half, :rows, mine]
                x = jnp.concatenate([agg[1, :, at], state], axis=1)
                xhat, inv = forward(1, x)
                y, s = activate(1, xhat)
                final_buf[:, at] = (state.astype(F32) + y * s).astype(BF16)
                up = cot_buf[:, at].astype(F32) * (1.0 / queries)
                both = backward(1, up, x, xhat, inv, y, s)
                dagg[:, part * breadth : (part + 1) * breadth] = both[:, :breadth]
                g1[:, at] = up + both[:, breadth:]
            edge_products(kept1, slice(None), 1)

            g1[:, wide] += dot(hot_t[:rows, :], contrib[...])
            stage[2, half, :, cols] = dot(hot_t[rows:, :], contrib[...]).astype(BF16)

        send(2, half)
        write_back(half).start()

    def gradients(layer):
        ar_stage[layer, :rel_rows, :] = dot(rel_t[...], per_edge[layer].astype(BF16)).astype(BF16)
        for part in range(2):
            first = rel_rows + part * breadth
            ar_stage[layer, first : first + breadth, :] = jnp.transpose(
                grad_w[layer, :, part * breadth : (part + 1) * breadth]
            ).astype(BF16)
        first = rel_rows + 2 * breadth
        ar_stage[layer, first : first + 16, :] = jnp.concatenate(
            [grad_b[layer], grad_g[layer]], axis=0
        ).astype(BF16)
        ar_stage[layer, first + 16 :, :] = jnp.zeros(
            (parts * chunk - first - 16, breadth), BF16
        )

    def scatter_sum(layer, i):
        peer = lax.rem(me + i, parts)
        return pltpu.make_async_remote_copy(
            src_ref=ar_stage.at[layer, pl.ds(pl.multiple_of(peer * chunk, 16), chunk)],
            dst_ref=ar_one.at[layer, me],
            send_sem=ar_send.at[layer, 0, i],
            recv_sem=ar_recv.at[layer, 0, i],
            device_id={"dom": peer},
            device_id_type=MESH,
        )

    def across(layer, i):
        return pltpu.make_async_remote_copy(
            src_ref=ar_two_stage.at[layer],
            dst_ref=ar_two.at[layer, meq],
            send_sem=ar_send_q.at[layer, i],
            recv_sem=ar_recv_q.at[layer, i],
            device_id={"qgrp": lax.rem(meq + i, groups)},
            device_id_type=MESH,
        )

    def spread(layer, i):
        return pltpu.make_async_remote_copy(
            src_ref=ar_three_stage.at[layer],
            dst_ref=ar_three.at[layer, pl.ds(pl.multiple_of(me * chunk, 16), chunk)],
            send_sem=ar_send.at[layer, 1, i],
            recv_sem=ar_recv.at[layer, 1, i],
            device_id={"dom": lax.rem(me + i, parts)},
            device_id_type=MESH,
        )

    def each(count, make, method):
        @pl.loop(1, count)
        def _(i):
            getattr(make(i), method)()

    def reduce_first(layer):
        ar_one[layer, me] = ar_stage[layer, pl.ds(pl.multiple_of(me * chunk, 16), chunk), :]
        each(parts, functools.partial(scatter_sum, layer), "start")

    def reduce_second(layer):
        each(parts, functools.partial(scatter_sum, layer), "wait_recv")
        total = ar_one[layer, 0].astype(F32)
        for p in range(1, parts):
            total = total + ar_one[layer, p].astype(F32)
        ar_two_stage[layer] = total.astype(BF16)
        ar_two[layer, meq] = total.astype(BF16)
        each(groups, functools.partial(across, layer), "start")

    def reduce_third(layer):
        each(groups, functools.partial(across, layer), "wait_recv")
        total = ar_two[layer, 0].astype(F32)
        for p in range(1, groups):
            total = total + ar_two[layer, p].astype(F32)
        ar_three_stage[layer] = total.astype(BF16)
        ar_three[layer, pl.ds(pl.multiple_of(me * chunk, 16), chunk), :] = total.astype(BF16)
        each(parts, functools.partial(spread, layer), "start")

    def reduce_finish(layer):
        each(parts, functools.partial(spread, layer), "wait_recv")
        grads_ref[layer] = ar_three[layer]
        each(parts, functools.partial(scatter_sum, layer), "wait_send")
        each(groups, functools.partial(across, layer), "wait_send")
        each(parts, functools.partial(spread, layer), "wait_send")

    gradients(1)
    reduce_first(1)

    for half in range(2):
        arrive(2, half)

        @pl.loop(0, blocks)
        def _(c):
            cols = pl.ds(pl.multiple_of(c * WIDE, WIDE), WIDE)
            wide = pl.ds(pl.multiple_of(half * half_cols + c * WIDE, WIDE), WIDE)
            g1[:, wide] += dot(pick_t[...], back_in[half, :, cols])
            for part in range(WIDE // breadth):
                at = pl.ds(
                    pl.multiple_of(half * half_cols + c * WIDE + part * breadth, breadth), breadth
                )
                x = jnp.concatenate([agg[0, :, at], h_ref[:, at]], axis=1)
                xhat = xhat0[:, at]
                y, s = activate(0, xhat)
                both = backward(0, g1[:, at], x, xhat, inv0[:, at], y, s)
                dagg[:, part * breadth : (part + 1) * breadth] = both[:, :breadth]
            edge_products(kept0, wide, 0)

        if half == 0:
            reduce_second(1)
        else:
            reduce_third(1)

    gradients(0)
    reduce_first(0)
    reduce_second(0)
    reduce_third(0)
    reduce_finish(1)
    reduce_finish(0)
    for step in range(3):
        for half in range(2):
            sent(step, half)
    for half in range(2):
        write_back(half).wait()


def unpack(
    final_in,
    grads_in,
    final_out,
    gm_ref,
    gs_ref,
    gb_ref,
    gg_ref,
    gr_ref,
    copy_sem,
):
    whole = pltpu.make_async_copy(final_in, final_out, copy_sem)
    whole.start()
    breadth = gm_ref.shape[1]
    rel_count = gr_ref.shape[0]
    rel_rows = -(-rel_count // 128) * 128
    for layer in range(2):
        gr_ref[:, layer, :] = grads_in[layer, :rel_count, :].astype(F32)
        gm_ref[layer] = grads_in[layer, rel_rows : rel_rows + breadth, :].astype(F32)
        gs_ref[layer] = grads_in[layer, rel_rows + breadth : rel_rows + 2 * breadth, :].astype(F32)
        first = rel_rows + 2 * breadth
        small = grads_in[layer, first : first + 16, :].astype(F32)
        gb_ref[layer : layer + 1, :] = jnp.sum(small[:8], axis=0, keepdims=True)
        gg_ref[layer : layer + 1, :] = jnp.sum(small[8:], axis=0, keepdims=True)
    whole.wait()


def local(
    parts,
    groups,
    pair_state,
    cotangent,
    msg_weight,
    self_weight,
    pre_bias,
    norm_gain,
    rel_embed,
    rel_ids,
    neighbours,
    border,
    send_list,
):
    rows, features = pair_state.shape
    degree = neighbours.shape[1]
    layers, rel_count, breadth = rel_embed.shape
    slots = parts * 8
    half_cols = features // 2
    edges = rows * degree
    rel_rows = -(-rel_count // 128) * 128
    chunk = -(-(rel_rows + 2 * breadth + 16) // (parts * 16)) * 16
    total = parts * chunk
    vmem = pl.BlockSpec(memory_space=pltpu.VMEM)
    anywhere = pl.BlockSpec(memory_space=pl.ANY)
    grads_shape = jax.ShapeDtypeStruct((layers, total, breadth), BF16)
    out_shape = [
        jax.ShapeDtypeStruct((rows, features), BF16),
        jax.ShapeDtypeStruct((layers, breadth, breadth), F32),
        jax.ShapeDtypeStruct((layers, breadth, breadth), F32),
        jax.ShapeDtypeStruct((layers, breadth), F32),
        jax.ShapeDtypeStruct((layers, breadth), F32),
        jax.ShapeDtypeStruct((rel_count, layers, breadth), F32),
    ]
    scratch = [
        pltpu.VMEM((layers, 2, rows + slots, half_cols), BF16),
        pltpu.VMEM((edges, rows + slots), BF16),
        pltpu.VMEM((rows + slots, edges), BF16),
        pltpu.VMEM((rel_rows, edges), BF16),
        pltpu.VMEM((edges, layers * breadth), BF16),
        pltpu.VMEM((rel_rows, layers * breadth), BF16),
        pltpu.VMEM((layers, 2 * breadth, breadth), BF16),
        pltpu.VMEM((slots, rows), BF16),
        pltpu.VMEM((rows, slots), BF16),
        pltpu.VMEM((edges, features), BF16),
        pltpu.VMEM((edges, WIDE), BF16),
        pltpu.VMEM((edges, WIDE), BF16),
        pltpu.VMEM((rows, features), F32),
        pltpu.VMEM((rows, features), F32),
        pltpu.VMEM((rows, features), F32),
        pltpu.VMEM((layers, rows, features), BF16),
        pltpu.VMEM((rows, WIDE), F32),
        pltpu.VMEM((layers, edges, breadth), F32),
        pltpu.VMEM((layers, breadth, 2 * breadth), F32),
        pltpu.VMEM((layers, 8, breadth), F32),
        pltpu.VMEM((layers, 8, breadth), F32),
        pltpu.VMEM((3, 2, slots, half_cols), BF16),
        pltpu.VMEM((2, slots, half_cols), BF16),
        pltpu.VMEM((layers, total, breadth), BF16),
        pltpu.VMEM((layers, parts, chunk, breadth), BF16),
        pltpu.VMEM((layers, chunk, breadth), BF16),
        pltpu.VMEM((layers, groups, chunk, breadth), BF16),
        pltpu.VMEM((layers, chunk, breadth), BF16),
        pltpu.VMEM((layers, total, breadth), BF16),
        pltpu.SemaphoreType.DMA((3, 2, parts)),
        pltpu.SemaphoreType.DMA((3, 2, parts)),
        pltpu.SemaphoreType.DMA((layers, 2, parts)),
        pltpu.SemaphoreType.DMA((layers, 2, parts)),
        pltpu.SemaphoreType.DMA((layers, groups)),
        pltpu.SemaphoreType.DMA((layers, groups)),
        pltpu.VMEM((rows, features), BF16),
        pltpu.VMEM((rows, features), BF16),
        pltpu.SemaphoreType.DMA((3,)),
    ]
    final, grads = pl.pallas_call(
        functools.partial(kernel, parts, groups, chunk),
        out_shape=[out_shape[0], grads_shape],
        in_specs=[vmem, anywhere] + [vmem] * 9,
        out_specs=[anywhere, vmem],
        scratch_shapes=scratch,
        compiler_params=pltpu.CompilerParams(
            collective_id=0, has_side_effects=True, vmem_limit_bytes=67043328
        ),
        name="bellman_ford",
    )(
        pair_state,
        cotangent,
        msg_weight,
        self_weight,
        pre_bias,
        norm_gain,
        jnp.transpose(rel_embed, (1, 0, 2)),
        rel_ids.T,
        neighbours.T,
        border,
        jnp.transpose(send_list, (0, 2, 1)),
    )
    final, gm, gs, gb, gg, gr = pl.pallas_call(
        unpack,
        out_shape=out_shape,
        in_specs=[vmem] * 2,
        out_specs=[anywhere] + [vmem] * 5,
        scratch_shapes=[pltpu.SemaphoreType.DMA],
        compiler_params=pltpu.CompilerParams(vmem_limit_bytes=67043328),
        name="unpack",
    )(final, grads)
    return final, gm, gs, gb, gg, jnp.transpose(gr, (1, 0, 2))


def solution(mesh):
    in_specs = (
        P("dom", "qgrp"),
        P("dom", "qgrp"),
        P(),
        P(),
        P(),
        P(),
        P(),
        P("dom", None),
        P("dom", None),
        P("dom", None),
        P("dom", None, None),
    )
    out_specs = (P("dom", "qgrp"), P(), P(), P(), P(), P())
    run = functools.partial(local, mesh.shape["dom"], mesh.shape["qgrp"])
    return jax.shard_map(run, mesh=mesh, in_specs=in_specs, out_specs=out_specs, check_vma=False)
```
